32 devices in a mesh: groups: 2 (over x), ctx: 16 (over z, y, core).
Axes of the slice: x: 2, y: 2, z: 4, core: 2. Of those that a mesh axis runs over, the one named last changes fastest.
Arguments:
- queries: bfloat16 [4096, 1024], P(('groups', 'ctx')), parts along dimension 0, may hold values from -27 to 27
- keys: bfloat16 [4096, 1024], P(('groups', 'ctx')), parts along dimension 0, may hold values from -6 to 6
- values: bfloat16 [4096, 1024], P(('groups', 'ctx')), parts along dimension 0, may hold values from -6 to 6
- resid: bfloat16 [4096, 2048], P(('groups', 'ctx')), parts along dimension 0, may hold values from -6 to 6
- out_proj: bfloat16 [1024, 2048], replicated, may hold values from -0.1875 to 0.1875
- norm_gain: float32 [2048], replicated, may hold values from 0.25 to 1.75
- up_proj: bfloat16 [2048, 4096], P(None, 'ctx'), may hold values from -0.125 to 0.125
- down_proj: bfloat16 [2048, 4096], P(None, 'ctx'), may hold values from -0.09375 to 0.09375
- router: bfloat16 [2048, 2], replicated, may hold values from -0.125 to 0.125
- expert_ids: int32 [4096, 1], P(('groups', 'ctx')), parts along dimension 0, may hold values from 0 to 1; in each aligned block of 128 rows (0 to 127, 128 to 255, ...) at most 80 rows name the same one
- expert_in: bfloat16 [16, 2048, 512], P('ctx'), may hold values from -0.125 to 0.125
- expert_out: bfloat16 [16, 512, 2048], P('ctx'), may hold values from -0.09375 to 0.09375
Outputs:
- layer_out: bfloat16 [4096, 2048], P(('groups', 'ctx')), parts along dimension 0
The draws below stay inside these ranges and needn't reach their ends.
There are 2 independent parts, one for each index of `groups`. The reference program is written for one: setup_inputs(seed, part) draws one part's arguments, and reference() takes and returns one part's arrays. A program takes and returns all parts, laid end to end along the dimension named above; an argument that names none is the same for every part. Nothing has to cross between parts.
Inputs may be any that keep to these rules, and one draw needn't show every extreme that they name: `expert_ids`: among the 128 tokens of one index of ctx, at most 80 name the same expert; in every draw some index of ctx has 80 tokens naming one expert.
All inputs are finite; a program needn't handle non-finite values.
Results may differ from the reference program's by a relative error of at most 0.0075.
Values may be sent and summed in bfloat16 or wider, within the bound.
No kernel may reach another device: no remote copies, remote signals or barrier semaphores. Data moves between devices by JAX's collectives and lax.ppermute only.
A program may use at most 192 MiB of HBM per device.

```python
import math
import jax
import jax.numpy as jnp
import numpy as np
from jax import lax

D = 2048
HEADS = 8
DH = 128
MLP_HID = 4096
EXP_HID = 4096
SPLIT = 8
TOK_DEV = 128
LIVE = 2
CAP = 80
SEQ = 2048
N_CTX = 16


def attention_draws(key):
    query_key = jax.random.fold_in(key, 11)
    keys_key = jax.random.fold_in(key, 12)
    width = HEADS * DH
    query_draw = jnp.clip(3.0 * jax.random.normal(query_key, (SEQ, width), jnp.float32), -18.0, 18.0)
    keys_draw = jnp.clip(jax.random.normal(keys_key, (SEQ, width), jnp.float32), -6.0, 6.0)
    return (query_draw, keys_draw)


def draw_queries(key, part):
    return attention_draws(key)[0].astype(jnp.bfloat16)


def draw_keys(key, part):
    return attention_draws(key)[1].astype(jnp.bfloat16)


def block_scale(own_key, shape, pieces, low, largest):
    def one(axis_at, blocks):
        draws = jax.random.uniform(jax.random.fold_in(jax.random.fold_in(own_key, 6), axis_at), (blocks,), jnp.float32, low / len(pieces), largest / len(pieces))
        return jnp.repeat(jnp.exp(draws), shape[axis_at] // blocks).reshape((-1,) + (1,) * (len(shape) - axis_at - 1))

    factor_of = one(*pieces[0])
    for cut in pieces[1:]:
        factor_of = factor_of * one(*cut)
    return factor_of


def routed_block(own_key, own, number, rows, number_of, top, reach, skew):
    order = jax.random.permutation(own_key, number_of)
    packed, ordinary = shares(number_of, rows * top, reach, skew, True), shares(number_of, rows * top, reach, skew, False)
    places = jnp.arange(number_of)

    def named(lengths, offset_by):
        used = int((lengths > 0).sum())
        fixed = max(1, used // 4)
        shifted = fixed + (places - fixed + offset_by * (used - fixed)) % max(1, number_of - fixed)
        return jnp.zeros((number_of,), jnp.int32).at[order[jnp.where(places < fixed, places, shifted)]].set(jnp.asarray(lengths, jnp.int32))

    lengths = jnp.where(number % 4 == 0, named(packed, number // 4), named(ordinary, number - number // 4 - 1))
    mixed = jax.random.permutation(jax.random.fold_in(own, 3), number_of)
    source_of, sink = mixed[0:number_of // 2 * 2:2], mixed[1:number_of // 2 * 2:2]
    slack = jnp.minimum(lengths[source_of] - 1, reach - lengths[sink]) // 2
    slack = jnp.where((source_of == order[0]) | (sink == order[0]) | (lengths[sink] == 0), 0, jnp.maximum(slack, 0))
    shifted = jax.random.randint(jax.random.fold_in(own, 4), (number_of // 2,), 0, 1 << 20) % (slack + 1)
    lengths = lengths.at[source_of].add(-shifted).at[sink].add(shifted)
    labels = jnp.searchsorted(jnp.cumsum(lengths), jnp.arange(rows * top), side="right").astype(jnp.int32)
    grid = labels.reshape(top, rows).T
    grid = grid[jax.random.permutation(jax.random.fold_in(own, 1), rows)]
    offset_by = jax.random.randint(jax.random.fold_in(own, 2), (rows, 1), 0, top)
    return jnp.take_along_axis(grid, (jnp.arange(top)[None, :] + offset_by) % top, axis=1)


def shares(number_of, total, reach, slope, full):
    loads = [(1 << 20) // math.isqrt(standing ** slope) + 1 for standing in range(1, number_of + 1)]
    largest = reach if full else min(reach, max(-(-total // number_of), total * loads[0] // sum(loads)))
    least = 1 if total - largest >= number_of - 1 else 0
    counts, spare = [largest] + [least] * (number_of - 1), total - largest - least * (number_of - 1)
    while spare > 0:
        movable = [i for i in range(1, number_of) if counts[i] < largest] or [i for i in range(1, number_of) if counts[i] < reach]
        mass, remaining = sum([loads[i] for i in movable]), spare
        for i in movable:
            addition = min(reach - counts[i], max(1, remaining * loads[i] // mass), spare)
            counts[i] = counts[i] + addition
            spare = spare - addition
    return np.array(counts)


def noise(own_key, extent, deviation, most, shards=(), kind=jnp.bfloat16):
    loudness = block_scale(own_key, extent, shards, -0.22, 0.18) if shards else 1.0
    entries = jax.random.normal(own_key, extent, jnp.float32) * deviation * loudness
    return jnp.minimum(jnp.maximum(entries, -most), most).astype(kind)


def setup_inputs(seed: int = 0, part: int = 0) -> dict:
    splits = jax.random.split(jax.random.key(seed), 13)
    part_keys = jax.random.split(jax.random.fold_in(splits[12], part), 13)
    queries = draw_queries(jax.random.fold_in(jax.random.fold_in(splits[12], part), 71), part)
    keys = draw_keys(jax.random.fold_in(jax.random.fold_in(splits[12], part), 71), part)
    values = noise(part_keys[2], (SEQ, HEADS * DH), 1.0, 6.0, ((0, 16),))
    resid = noise(part_keys[3], (SEQ, D), 1.0, 6.0, ((0, 16),))
    out_proj = noise(splits[4], (HEADS * DH, D), (HEADS * DH) ** -0.5, 0.1875)
    norm_gain = jnp.clip(1.0 + 0.15 * jax.random.normal(splits[5], (D,), jnp.float32), 0.25, 1.75)
    up_proj = noise(splits[6], (D, MLP_HID), D ** -0.5, 0.125, ((1, 16),))
    down_proj = noise(splits[7], (D, MLP_HID), MLP_HID ** -0.5, 0.09375, ((1, 16),))
    router = noise(splits[8], (D, LIVE), D ** -0.5, 0.125)
    expert_ids_keys = jax.random.split(jax.random.fold_in(part_keys[9], 1), SEQ // TOK_DEV)
    expert_ids_turns = jax.random.permutation(jax.random.fold_in(part_keys[9], 3), SEQ // TOK_DEV)
    expert_ids = jax.vmap(lambda own, number: routed_block(jax.random.fold_in(part_keys[9], 2), own, number, TOK_DEV, LIVE, 1, CAP, 2))(expert_ids_keys, expert_ids_turns).reshape((SEQ, 1))
    expert_in = noise(splits[10], (SPLIT * LIVE, D, EXP_HID // SPLIT), D ** -0.5, 0.125, ((0, 16),))
    expert_out = noise(splits[11], (SPLIT * LIVE, EXP_HID // SPLIT, D), EXP_HID ** -0.5, 0.09375, ((0, 16),))
    return dict(queries=queries, keys=keys, values=values, resid=resid, out_proj=out_proj, norm_gain=norm_gain, up_proj=up_proj, down_proj=down_proj, router=router, expert_ids=expert_ids, expert_in=expert_in, expert_out=expert_out)


NEG_FILL = -1e+30
EPSILON = 1e-06

def reference(queries, keys, values, resid, out_proj, norm_gain, up_proj, down_proj, router, expert_ids, expert_in, expert_out):
    total_rows = queries.shape[0]
    key_heads = keys.astype(jnp.float32).reshape(total_rows, HEADS, DH)
    value_heads = values.astype(jnp.float32).reshape(total_rows, HEADS, DH)
    query_blocks = queries.reshape(N_CTX, TOK_DEV, HEADS, DH)
    key_positions = jnp.arange(total_rows, dtype=jnp.int32)

    def attend_block(operands):
        block_rows, block_index = operands
        scores = jnp.einsum('qhd,khd->hqk', block_rows.astype(jnp.float32), key_heads) * DH ** (-0.5)
        query_positions = block_index * TOK_DEV + jnp.arange(TOK_DEV, dtype=jnp.int32)
        visible = (key_positions[None, :] <= query_positions[:, None])[None]
        masked = jnp.where(visible, scores, NEG_FILL)
        row_max = lax.optimization_barrier(jnp.max(masked, axis=2))
        weights = jnp.where(visible, jnp.exp(masked - row_max[..., None]), 0.0)
        totals = lax.optimization_barrier(jnp.sum(weights, axis=2))
        numer = jnp.einsum('hqk,khd->hqd', weights.astype(jnp.bfloat16).astype(jnp.float32), value_heads)
        result = (numer / totals[..., None]).astype(jnp.bfloat16)
        return jnp.transpose(result, (1, 0, 2)).reshape(TOK_DEV, HEADS * DH)
    attn = lax.map(attend_block, (query_blocks, jnp.arange(N_CTX, dtype=jnp.int32))).reshape(total_rows, HEADS * DH)
    mixed = resid.astype(jnp.float32) + jnp.dot(attn, out_proj, preferred_element_type=jnp.float32)
    normed = (mixed * lax.rsqrt(lax.optimization_barrier(jnp.mean(mixed * mixed, axis=1, keepdims=True)) + EPSILON) * norm_gain).astype(jnp.bfloat16)
    chosen = expert_ids[:, 0]
    onehot = (chosen[:, None] == jnp.arange(LIVE, dtype=jnp.int32)[None, :]).astype(jnp.float32)
    logits = jnp.dot(normed, router, preferred_element_type=jnp.float32)
    gate = jax.nn.sigmoid(lax.optimization_barrier(jnp.sum(onehot * logits, axis=1)))
    block_units = EXP_HID // SPLIT
    mlp_units = MLP_HID // SPLIT
    full_in = jnp.transpose(expert_in.reshape(SPLIT, LIVE, D, block_units), (1, 2, 0, 3)).reshape(LIVE, D, EXP_HID)
    full_out = jnp.transpose(expert_out.reshape(SPLIT, LIVE, block_units, D), (1, 0, 2, 3)).reshape(LIVE, EXP_HID, D)
    grouped = onehot.reshape(N_CTX, TOK_DEV, LIVE)
    earlier = jnp.cumsum(grouped, axis=1) - grouped
    slot_index = lax.optimization_barrier(jnp.sum(earlier * grouped, axis=2)).reshape(total_rows).astype(jnp.int32)
    owner_index = (jnp.arange(total_rows, dtype=jnp.int32) // TOK_DEV).astype(jnp.int32)
    buffer_index = chosen * (N_CTX * CAP) + owner_index * CAP + slot_index
    buffer_rows = jnp.zeros((LIVE * N_CTX * CAP, D), jnp.bfloat16).at[buffer_index].set(normed)
    buffer_rows = buffer_rows.reshape(LIVE, N_CTX * CAP, D)
    gate_rows = jnp.zeros((LIVE * N_CTX * CAP,), jnp.float32).at[buffer_index].set(gate).reshape(LIVE, N_CTX * CAP)

    def apply_expert(operands):
        rows_in, gate_in, weight_in, weight_out = operands
        total = jnp.zeros((rows_in.shape[0], D), jnp.float32)
        for block in range(SPLIT):
            expert_low = block * block_units
            mlp_low = block * mlp_units
            expert_hidden = jax.nn.gelu(jnp.dot(rows_in, weight_in[:, expert_low:expert_low + block_units], preferred_element_type=jnp.float32)).astype(jnp.bfloat16)
            mlp_hidden = jax.nn.gelu(jnp.dot(rows_in, up_proj[:, mlp_low:mlp_low + mlp_units], preferred_element_type=jnp.float32)).astype(jnp.bfloat16)
            block_part = gate_in[:, None] * jnp.dot(expert_hidden, weight_out[expert_low:expert_low + block_units], preferred_element_type=jnp.float32)
            block_part = block_part + lax.dot_general(mlp_hidden, down_proj[:, mlp_low:mlp_low + mlp_units], (((1,), (1,)), ((), ())), preferred_element_type=jnp.float32)
            rounded = lax.optimization_barrier(block_part.astype(jnp.bfloat16))
            total = total + rounded.astype(jnp.float32)
        return total
    expert_rows = lax.map(apply_expert, (buffer_rows, gate_rows, full_in, full_out)).reshape(LIVE * N_CTX * CAP, D)
    mixture_part = expert_rows[buffer_index]
    return (mixed + mixture_part).astype(jnp.bfloat16)
```

```python
import jax
import jax.numpy as jnp
from jax import lax
from jax.experimental import pallas as pl
from jax.experimental.pallas import tpu as pltpu
from jax.sharding import PartitionSpec as P

DH = 128
SPLIT = 8


NEG_FILL = -1e30
EPSILON = 1e-06


def from_partner(array, axis, apart):
    return lax.ppermute(array, axis, [(i, i ^ 1 << apart) for i in range(lax.axis_size(axis))])


def update_state(state, query_rows, query_offset, key_block, value_block, key_offset):
    maxima, totals, numer = state
    count_query = query_rows.shape[0]
    count_keys = key_block.shape[0]
    head_count = query_rows.shape[1] // DH
    query_heads = query_rows.reshape(count_query, head_count, DH)
    key_heads = key_block.reshape(count_keys, head_count, DH)
    value_heads = value_block.reshape(count_keys, head_count, DH)
    scores = jnp.einsum(
        "qhd,khd->hqk", query_heads, key_heads, preferred_element_type=jnp.float32
    ) * DH ** (-0.5)
    query_positions = query_offset + jnp.arange(count_query, dtype=jnp.int32)
    key_positions = key_offset + jnp.arange(count_keys, dtype=jnp.int32)
    visible = (key_positions[None, :] <= query_positions[:, None])[None]
    masked = jnp.where(visible, scores, NEG_FILL)
    new_max = jnp.maximum(maxima, jnp.max(masked, axis=2))
    weights = jnp.where(visible, jnp.exp(masked - new_max[..., None]), 0.0)
    factor = jnp.exp(maxima - new_max)
    totals = totals * factor + jnp.sum(weights, axis=2)
    numer = numer * factor[..., None] + jnp.einsum(
        "hqk,khd->hqd",
        weights.astype(jnp.bfloat16),
        value_heads,
        preferred_element_type=jnp.float32,
    )
    return (new_max, totals, numer)


def attend(query_sets, keys, values):
    head_count = keys.shape[1] // DH
    initial = []
    for query_rows, query_offset in query_sets:
        count_query = query_rows.shape[0]
        initial.append(
            (
                jnp.full((head_count, count_query), NEG_FILL, jnp.float32),
                jnp.zeros((head_count, count_query), jnp.float32),
                jnp.zeros((head_count, count_query, DH), jnp.float32),
            )
        )
    states = tuple(initial)
    key_offset = jnp.int32(0)
    key_whole = lax.all_gather(keys, "ctx", axis=0, tiled=True)
    value_whole = lax.all_gather(values, "ctx", axis=0, tiled=True)
    total_keys = key_whole.shape[0]
    step_rows = min(total_keys, 1024)
    for begin in range(0, total_keys, step_rows):
        key_block = key_whole[begin : begin + step_rows]
        value_block = value_whole[begin : begin + step_rows]
        block_offset = key_offset + begin
        query_rows, query_offset = query_sets[0]
        needed = block_offset <= query_offset + query_rows.shape[0] - 1
        updated = [
            lax.cond(
                needed,
                lambda carried, rows_now=query_rows, offset_now=query_offset, keys_now=key_block, values_now=value_block, start_now=block_offset: update_state(
                    carried, rows_now, offset_now, keys_now, values_now, start_now
                ),
                lambda carried: carried,
                states[0],
            )
        ]
        states = tuple(updated)
    results = []
    for maxima, totals, numer in states:
        result = (numer / totals[..., None]).astype(jnp.bfloat16)
        results.append(
            jnp.transpose(result, (1, 0, 2)).reshape(result.shape[1], result.shape[0] * DH)
        )
    return results


def body(
    queries,
    keys,
    values,
    resid,
    out_proj,
    norm_gain,
    up_proj,
    down_proj,
    router,
    expert_ids,
    expert_in,
    expert_out,
):
    tok_rows = queries.shape[0]
    width = resid.shape[1]
    live_count = router.shape[1]
    ctx_count = lax.axis_size("ctx")
    device_index = lax.axis_index("ctx")
    base_offset = device_index * tok_rows
    attn = attend([(queries, base_offset)], keys, values)[0]
    mixed = resid.astype(jnp.float32) + jnp.dot(attn, out_proj, preferred_element_type=jnp.float32)
    normed = (
        mixed * lax.rsqrt(jnp.mean(mixed * mixed, axis=1, keepdims=True) + EPSILON) * norm_gain
    ).astype(jnp.bfloat16)
    mlp_blocks = jnp.stack([up_proj, down_proj], 0)
    for level in range(live_count.bit_length() - 1):
        other_block = from_partner(mlp_blocks, "ctx", level)
        mlp_blocks = jnp.concatenate([mlp_blocks, other_block], axis=2)
    slots_per = max(2, 5 * tok_rows // (4 * live_count))
    chosen = expert_ids[:, 0]
    onehot = (chosen[:, None] == jnp.arange(live_count, dtype=jnp.int32)[None, :]).astype(
        jnp.bfloat16
    )
    row_iota = jnp.arange(tok_rows, dtype=jnp.int32)
    strictly_lower = (row_iota[None, :] < row_iota[:, None]).astype(jnp.bfloat16)
    counts_before = jnp.dot(strictly_lower, onehot, preferred_element_type=jnp.float32)
    slot_index = jnp.sum(onehot.astype(jnp.float32) * counts_before, axis=1).astype(jnp.int32)
    target_slot = chosen * slots_per + slot_index
    dispatch_matrix = (
        jnp.arange(live_count * slots_per, dtype=jnp.int32)[:, None] == target_slot[None, :]
    ).astype(jnp.bfloat16)
    packed = jnp.dot(dispatch_matrix, normed, preferred_element_type=jnp.float32).astype(
        jnp.bfloat16
    )
    sending = jnp.broadcast_to(
        packed.reshape(1, live_count, slots_per, width), (SPLIT, live_count, slots_per, width)
    )
    sending = sending.reshape(ctx_count, 1, slots_per, width)
    own_expert = device_index % live_count
    router_column = lax.dynamic_slice_in_dim(router, own_expert, 1, 1)
    weight_in = expert_in[0]
    weight_out = expert_out[0]
    received = lax.all_to_all(sending, "ctx", split_axis=0, concat_axis=1, tiled=True)
    rows = received.reshape(-1, width)
    expert_hidden = jax.nn.gelu(
        jnp.dot(rows, weight_in, preferred_element_type=jnp.float32)
    ).astype(jnp.bfloat16)
    mlp_hidden = jax.nn.gelu(
        jnp.dot(rows, mlp_blocks[0], preferred_element_type=jnp.float32)
    ).astype(jnp.bfloat16)
    gate = jax.nn.sigmoid(jnp.dot(rows, router_column, preferred_element_type=jnp.float32))
    produced = gate * jnp.dot(expert_hidden, weight_out, preferred_element_type=jnp.float32)
    produced = produced + lax.dot_general(
        mlp_hidden, mlp_blocks[1], (((1,), (1,)), ((), ())), preferred_element_type=jnp.float32
    )
    came_back = lax.all_to_all(
        produced.astype(jnp.bfloat16).reshape(received.shape),
        "ctx",
        split_axis=1,
        concat_axis=0,
        tiled=True,
    )
    summed = jnp.sum(
        came_back.astype(jnp.float32).reshape(SPLIT, live_count * slots_per, width), axis=0
    )
    mixture_part = lax.dot_general(
        dispatch_matrix.astype(jnp.float32),
        summed,
        (((0,), (0,)), ((), ())),
        precision=lax.Precision.HIGHEST,
        preferred_element_type=jnp.float32,
    )
    return (mixed + mixture_part).astype(jnp.bfloat16)


def swap(array, mask):
    return lax.ppermute(array, "ctx", [(i, i ^ mask) for i in range(lax.axis_size("ctx"))])


def attention_kernel(core_ref, own_ref, other_ref, ids_ref, out_ref):
    core = core_ref[0]
    blocks, rows, _ = own_ref.shape
    row_at = lax.broadcasted_iota(jnp.int32, (rows, rows), 0)
    column_at = lax.broadcasted_iota(jnp.int32, (rows, rows), 1)
    causal = column_at <= row_at
    also = jnp.broadcast_to(core == 1, (rows, rows))
    contract = (((1,), (1,)), ((), ()))
    for block in range(blocks):
        query = own_ref[block, :, :DH]
        scores = []
        for ref, first, last_visible in ((own_ref, DH, causal), (other_ref, 0, also)):
            for at in range(block + 1):
                score = lax.dot_general(
                    query, ref[at, :, first : first + DH], contract, preferred_element_type=jnp.float32
                ) * DH ** (-0.5)
                if at == block:
                    score = jnp.where(last_visible, score, NEG_FILL)
                scores.append(score)
        peak = scores[0]
        for score in scores[1:]:
            peak = jnp.maximum(peak, score)
        row_max = jnp.max(peak, axis=1, keepdims=True)
        numer = jnp.zeros((rows, DH), jnp.float32)
        summed = jnp.zeros((rows, rows), jnp.float32)
        for at, score in enumerate(scores):
            weights = jnp.exp(score - row_max)
            summed = summed + weights
            if at <= block:
                value = own_ref[at, :, 2 * DH :]
            else:
                value = other_ref[at - block - 1, :, DH:]
            numer = numer + jnp.dot(
                weights.astype(jnp.bfloat16), value, preferred_element_type=jnp.float32
            )
        totals = jnp.sum(summed, axis=1, keepdims=True)
        out_ref[block, :rows, :] = (numer / totals).astype(jnp.bfloat16)
        out_ref[block, rows:, :] = ids_ref[...]


def attend_by_head(queries, keys, values, id_rows, groups, core):
    rows = queries.shape[0]
    heads = queries.shape[1] // DH
    packed = jnp.concatenate(
        [part.reshape(rows, heads, DH) for part in (queries, keys, values)], axis=2
    ).transpose(1, 0, 2)
    own = lax.all_to_all(
        packed, "ctx", split_axis=0, concat_axis=0, tiled=True, axis_index_groups=groups
    )
    other = swap(own[:, :, DH:], 1)
    out = pl.pallas_call(
        attention_kernel,
        out_shape=jax.ShapeDtypeStruct((heads, rows + id_rows.shape[0], DH), jnp.bfloat16),
        in_specs=[pl.BlockSpec(memory_space=pltpu.SMEM)] + [pl.BlockSpec(memory_space=pltpu.VMEM)] * 3,
        out_specs=pl.BlockSpec(memory_space=pltpu.VMEM),
        cost_estimate=pl.CostEstimate(flops=10**9, bytes_accessed=2 * 10**6, transcendentals=10**6),
    )(core.reshape(1), own, other, id_rows)
    return lax.all_to_all(
        out, "ctx", split_axis=0, concat_axis=0, tiled=True, axis_index_groups=groups
    )


def mixture_kernel(
    first_ref, second_ref, mine_ref, router_ref, *rest
):
    weight_refs, out_refs, scratch, sems = rest[:8], rest[8:10], rest[10:18], rest[18]
    copies = [
        pltpu.make_async_copy(source, target, sems.at[at])
        for at, (source, target) in enumerate(zip(weight_refs, scratch))
    ]
    for copy in copies:
        copy.start()
    rows = first_ref.shape[0]
    width = first_ref.shape[1]
    normed = jnp.concatenate([first_ref[...], second_ref[...]], axis=0)
    mine = jnp.concatenate([mine_ref[0], mine_ref[1]], axis=0)
    column = jnp.where(mine > 0, router_ref[0:1, :], router_ref[1:2, :])
    logits = jnp.sum(normed.astype(jnp.float32) * column, axis=1, keepdims=True)
    gate = jax.nn.sigmoid(logits)

    def hidden(weights):
        return jax.nn.gelu(jnp.dot(normed, weights[...], preferred_element_type=jnp.float32))

    up_a, up_b, in_a, in_b, down_a, down_b, out_a, out_b = scratch
    copies[0].wait()
    mlp_a = hidden(up_a).astype(jnp.bfloat16)
    copies[1].wait()
    mlp_b = hidden(up_b).astype(jnp.bfloat16)
    copies[2].wait()
    exp_a = jnp.where(mine > 0, hidden(in_a), 0.0).astype(jnp.bfloat16)
    copies[3].wait()
    exp_b = jnp.where(mine > 0, 0.0, hidden(in_b)).astype(jnp.bfloat16)
    for copy in copies[4:]:
        copy.wait()
    contract = (((1,), (1,)), ((), ()))
    step = min(width, 512)
    for begin in range(0, width, step):
        span = slice(begin, begin + step)
        part = gate * (
            jnp.dot(exp_a, out_a[:, span], preferred_element_type=jnp.float32)
            + jnp.dot(exp_b, out_b[:, span], preferred_element_type=jnp.float32)
        )
        part = part + (
            lax.dot_general(mlp_a, down_a[span, :], contract, preferred_element_type=jnp.float32)
            + lax.dot_general(mlp_b, down_b[span, :], contract, preferred_element_type=jnp.float32)
        )
        part = part.astype(jnp.bfloat16)
        out_refs[0][:, span] = part[:rows]
        out_refs[1][:, span] = part[rows:]


def mixture_part(first, second, mine, router_rows, weights):
    rows, width = first.shape
    vmem, hbm = pl.BlockSpec(memory_space=pltpu.VMEM), pl.BlockSpec(memory_space=pl.ANY)
    flops = 4 * rows * 2 * width * sum(w.size // width for w in weights[:4])
    return pl.pallas_call(
        mixture_kernel,
        out_shape=[jax.ShapeDtypeStruct((rows, width), jnp.bfloat16)] * 2,
        in_specs=[vmem] * 4 + [hbm] * 8,
        out_specs=[vmem] * 2,
        scratch_shapes=[pltpu.VMEM(w.shape, w.dtype) for w in weights]
        + [pltpu.SemaphoreType.DMA((8,))],
        compiler_params=pltpu.CompilerParams(vmem_limit_bytes=40 * 2**20),
        cost_estimate=pl.CostEstimate(
            flops=flops, bytes_accessed=sum(2 * w.size for w in weights), transcendentals=0
        ),
    )(first, second, mine, router_rows, *weights)


def body_by_pairs(
    queries,
    keys,
    values,
    resid,
    out_proj,
    norm_gain,
    up_proj,
    down_proj,
    router,
    expert_ids,
    expert_in,
    expert_out,
):
    rows, width = resid.shape
    ctx_count = lax.axis_size("ctx")
    device_index = lax.axis_index("ctx")
    core = device_index % 2
    groups = [list(range(parity, ctx_count, 2)) for parity in range(2)]
    weights_own = (up_proj, expert_in[0], down_proj, expert_out[0])
    weights_other = tuple(swap(array, 1) for array in weights_own)
    weights = tuple(w for pair in zip(weights_own, weights_other) for w in pair)
    id_rows = jnp.broadcast_to(expert_ids[:, 0].astype(jnp.bfloat16)[None, :], (16, rows))
    heads_back = attend_by_head(queries, keys, values, id_rows, groups, core)
    attn = heads_back[:, :rows, :].transpose(1, 0, 2).reshape(rows, -1)
    mixed = resid.astype(jnp.float32) + jnp.dot(attn, out_proj, preferred_element_type=jnp.float32)
    normed = (
        mixed * lax.rsqrt(jnp.mean(mixed * mixed, axis=1, keepdims=True) + EPSILON) * norm_gain
    ).astype(jnp.bfloat16)
    mine = (heads_back[:, rows, :] == core.astype(jnp.bfloat16)).astype(jnp.float32)[:, :, None]
    router_rows = router.astype(jnp.float32).T
    router_rows = jnp.where(core == 0, router_rows, router_rows[::-1])

    far_first = [4 * at for at in range(ctx_count // 4 - 1, 0, -1)]
    near = {0: normed}
    for offset in far_first:
        near[offset] = swap(normed, offset)
    across = {offset: swap(near[offset], 2) for offset in [0] + far_first}
    total = mixed
    for offset in far_first + [0]:
        both = jnp.stack(
            [
                lax.dynamic_index_in_dim(mine, (device_index ^ mask) // 2, 0, keepdims=False)
                for mask in (offset, offset | 2)
            ],
            0,
        )
        part, part_across = mixture_part(near[offset], across[offset], both, router_rows, weights)
        summed = part.astype(jnp.float32) + swap(part_across, 2).astype(jnp.float32)
        if offset:
            summed = swap(summed.astype(jnp.bfloat16), offset).astype(jnp.float32)
        total = total + summed
    return total.astype(jnp.bfloat16)


def solution(mesh):
    ctx_count = mesh.shape["ctx"]

    def chosen(*args):
        queries, router = args[0], args[8]
        by_pairs = (
            router.shape[1] == 2
            and ctx_count == 2 * SPLIT
            and queries.shape[1] == ctx_count // 2 * DH
            and ctx_count % 4 == 0
            and ctx_count & (ctx_count - 1) == 0
        )
        return (body_by_pairs if by_pairs else body)(*args)

    placed = (
        P(("groups", "ctx"), None),
        P(("groups", "ctx"), None),
        P(("groups", "ctx"), None),
        P(("groups", "ctx"), None),
        P(),
        P(),
        P(None, "ctx"),
        P(None, "ctx"),
        P(),
        P(("groups", "ctx"), None),
        P("ctx", None, None),
        P("ctx", None, None),
    )
    return jax.shard_map(
        chosen, mesh=mesh, in_specs=placed, out_specs=P(("groups", "ctx"), None), check_vma=False
    )
```

```python
import functools
import jax
import jax.numpy as jnp
from jax import lax
from jax.experimental import pallas as pl
from jax.experimental.pallas import tpu as pltpu
from jax.sharding import PartitionSpec as P

DH = 128
SPLIT = 8


NEG_FILL = -1e30
EPSILON = 1e-06


def from_partner(array, axis, apart):
    return lax.ppermute(array, axis, [(i, i ^ 1 << apart) for i in range(lax.axis_size(axis))])


def update_state(state, query_rows, query_offset, key_block, value_block, key_offset):
    maxima, totals, numer = state
    count_query = query_rows.shape[0]
    count_keys = key_block.shape[0]
    head_count = query_rows.shape[1] // DH
    query_heads = query_rows.reshape(count_query, head_count, DH)
    key_heads = key_block.reshape(count_keys, head_count, DH)
    value_heads = value_block.reshape(count_keys, head_count, DH)
    scores = jnp.einsum(
        "qhd,khd->hqk", query_heads, key_heads, preferred_element_type=jnp.float32
    ) * DH ** (-0.5)
    query_positions = query_offset + jnp.arange(count_query, dtype=jnp.int32)
    key_positions = key_offset + jnp.arange(count_keys, dtype=jnp.int32)
    visible = (key_positions[None, :] <= query_positions[:, None])[None]
    masked = jnp.where(visible, scores, NEG_FILL)
    new_max = jnp.maximum(maxima, jnp.max(masked, axis=2))
    weights = jnp.where(visible, jnp.exp(masked - new_max[..., None]), 0.0)
    factor = jnp.exp(maxima - new_max)
    totals = totals * factor + jnp.sum(weights, axis=2)
    numer = numer * factor[..., None] + jnp.einsum(
        "hqk,khd->hqd",
        weights.astype(jnp.bfloat16),
        value_heads,
        preferred_element_type=jnp.float32,
    )
    return (new_max, totals, numer)


def attend(query_sets, keys, values):
    head_count = keys.shape[1] // DH
    initial = []
    for query_rows, query_offset in query_sets:
        count_query = query_rows.shape[0]
        initial.append(
            (
                jnp.full((head_count, count_query), NEG_FILL, jnp.float32),
                jnp.zeros((head_count, count_query), jnp.float32),
                jnp.zeros((head_count, count_query, DH), jnp.float32),
            )
        )
    states = tuple(initial)
    key_offset = jnp.int32(0)
    key_whole = lax.all_gather(keys, "ctx", axis=0, tiled=True)
    value_whole = lax.all_gather(values, "ctx", axis=0, tiled=True)
    total_keys = key_whole.shape[0]
    step_rows = min(total_keys, 1024)
    for begin in range(0, total_keys, step_rows):
        key_block = key_whole[begin : begin + step_rows]
        value_block = value_whole[begin : begin + step_rows]
        block_offset = key_offset + begin
        query_rows, query_offset = query_sets[0]
        needed = block_offset <= query_offset + query_rows.shape[0] - 1
        updated = [
            lax.cond(
                needed,
                lambda carried, rows_now=query_rows, offset_now=query_offset, keys_now=key_block, values_now=value_block, start_now=block_offset: update_state(
                    carried, rows_now, offset_now, keys_now, values_now, start_now
                ),
                lambda carried: carried,
                states[0],
            )
        ]
        states = tuple(updated)
    results = []
    for maxima, totals, numer in states:
        result = (numer / totals[..., None]).astype(jnp.bfloat16)
        results.append(
            jnp.transpose(result, (1, 0, 2)).reshape(result.shape[1], result.shape[0] * DH)
        )
    return results


def body(
    queries,
    keys,
    values,
    resid,
    out_proj,
    norm_gain,
    up_proj,
    down_proj,
    router,
    expert_ids,
    expert_in,
    expert_out,
):
    tok_rows = queries.shape[0]
    width = resid.shape[1]
    live_count = router.shape[1]
    ctx_count = lax.axis_size("ctx")
    device_index = lax.axis_index("ctx")
    base_offset = device_index * tok_rows
    attn = attend([(queries, base_offset)], keys, values)[0]
    mixed = resid.astype(jnp.float32) + jnp.dot(attn, out_proj, preferred_element_type=jnp.float32)
    normed = (
        mixed * lax.rsqrt(jnp.mean(mixed * mixed, axis=1, keepdims=True) + EPSILON) * norm_gain
    ).astype(jnp.bfloat16)
    mlp_blocks = jnp.stack([up_proj, down_proj], 0)
    for level in range(live_count.bit_length() - 1):
        other_block = from_partner(mlp_blocks, "ctx", level)
        mlp_blocks = jnp.concatenate([mlp_blocks, other_block], axis=2)
    slots_per = max(2, 5 * tok_rows // (4 * live_count))
    chosen = expert_ids[:, 0]
    onehot = (chosen[:, None] == jnp.arange(live_count, dtype=jnp.int32)[None, :]).astype(
        jnp.bfloat16
    )
    row_iota = jnp.arange(tok_rows, dtype=jnp.int32)
    strictly_lower = (row_iota[None, :] < row_iota[:, None]).astype(jnp.bfloat16)
    counts_before = jnp.dot(strictly_lower, onehot, preferred_element_type=jnp.float32)
    slot_index = jnp.sum(onehot.astype(jnp.float32) * counts_before, axis=1).astype(jnp.int32)
    target_slot = chosen * slots_per + slot_index
    dispatch_matrix = (
        jnp.arange(live_count * slots_per, dtype=jnp.int32)[:, None] == target_slot[None, :]
    ).astype(jnp.bfloat16)
    packed = jnp.dot(dispatch_matrix, normed, preferred_element_type=jnp.float32).astype(
        jnp.bfloat16
    )
    sending = jnp.broadcast_to(
        packed.reshape(1, live_count, slots_per, width), (SPLIT, live_count, slots_per, width)
    )
    sending = sending.reshape(ctx_count, 1, slots_per, width)
    own_expert = device_index % live_count
    router_column = lax.dynamic_slice_in_dim(router, own_expert, 1, 1)
    weight_in = expert_in[0]
    weight_out = expert_out[0]
    received = lax.all_to_all(sending, "ctx", split_axis=0, concat_axis=1, tiled=True)
    rows = received.reshape(-1, width)
    expert_hidden = jax.nn.gelu(
        jnp.dot(rows, weight_in, preferred_element_type=jnp.float32)
    ).astype(jnp.bfloat16)
    mlp_hidden = jax.nn.gelu(
        jnp.dot(rows, mlp_blocks[0], preferred_element_type=jnp.float32)
    ).astype(jnp.bfloat16)
    gate = jax.nn.sigmoid(jnp.dot(rows, router_column, preferred_element_type=jnp.float32))
    produced = gate * jnp.dot(expert_hidden, weight_out, preferred_element_type=jnp.float32)
    produced = produced + lax.dot_general(
        mlp_hidden, mlp_blocks[1], (((1,), (1,)), ((), ())), preferred_element_type=jnp.float32
    )
    came_back = lax.all_to_all(
        produced.astype(jnp.bfloat16).reshape(received.shape),
        "ctx",
        split_axis=1,
        concat_axis=0,
        tiled=True,
    )
    summed = jnp.sum(
        came_back.astype(jnp.float32).reshape(SPLIT, live_count * slots_per, width), axis=0
    )
    mixture_part = lax.dot_general(
        dispatch_matrix.astype(jnp.float32),
        summed,
        (((0,), (0,)), ((), ())),
        precision=lax.Precision.HIGHEST,
        preferred_element_type=jnp.float32,
    )
    return (mixed + mixture_part).astype(jnp.bfloat16)


def swap(array, mask):
    return lax.ppermute(array, "ctx", [(i, i ^ mask) for i in range(lax.axis_size("ctx"))])


VMEM = pl.BlockSpec(memory_space=pltpu.VMEM)
SMEM = pl.BlockSpec(memory_space=pltpu.SMEM)


def call(kernel, outs, specs, flops, mib, *operands):
    return pl.pallas_call(
        kernel,
        out_shape=outs,
        in_specs=specs,
        out_specs=[VMEM] * len(outs),
        compiler_params=pltpu.CompilerParams(vmem_limit_bytes=mib * 2**20),
        cost_estimate=pl.CostEstimate(
            flops=flops,
            bytes_accessed=sum(x.size * x.dtype.itemsize for x in operands),
            transcendentals=0,
        ),
    )(*operands)


def pack_kernel(query_ref, key_ref, value_ref, out_ref):
    for head in range(out_ref.shape[0]):
        columns = slice(head * DH, (head + 1) * DH)
        for at, ref in enumerate((query_ref, key_ref, value_ref)):
            out_ref[head, :, at * DH : (at + 1) * DH] = ref[:, columns]


def attention_kernel(core_ref, own_ref, other_ref, ids_ref, out_ref):
    core = core_ref[0]
    blocks, rows, _ = own_ref.shape
    row_at = lax.broadcasted_iota(jnp.int32, (rows, rows), 0)
    column_at = lax.broadcasted_iota(jnp.int32, (rows, rows), 1)
    causal = column_at <= row_at
    also = jnp.broadcast_to(core == 1, (rows, rows))
    contract = (((1,), (1,)), ((), ()))
    id_rows = jnp.broadcast_to(
        ids_ref[...].astype(jnp.float32), (out_ref.shape[1] - rows, rows)
    ).astype(jnp.bfloat16)
    for block in range(blocks):
        query = own_ref[block, :, :DH]
        scores = []
        for ref, last_visible in ((own_ref, causal), (other_ref, also)):
            for at in range(block + 1):
                score = lax.dot_general(
                    query,
                    ref[at, :, DH : 2 * DH],
                    contract,
                    preferred_element_type=jnp.float32,
                ) * DH ** (-0.5)
                if at == block:
                    score = jnp.where(last_visible, score, NEG_FILL)
                scores.append(score)
        peak = scores[0]
        for score in scores[1:]:
            peak = jnp.maximum(peak, score)
        row_max = jnp.max(peak, axis=1, keepdims=True)
        numer = jnp.zeros((rows, DH), jnp.float32)
        summed = jnp.zeros((rows, rows), jnp.float32)
        for at, score in enumerate(scores):
            weights = jnp.exp(score - row_max)
            summed = summed + weights
            ref = own_ref if at <= block else other_ref
            numer = numer + jnp.dot(
                weights.astype(jnp.bfloat16),
                ref[at % (block + 1), :, 2 * DH :],
                preferred_element_type=jnp.float32,
            )
        totals = jnp.sum(summed, axis=1, keepdims=True)
        out_ref[block, :rows, :] = (numer / totals).astype(jnp.bfloat16)
        out_ref[block, rows:, :] = id_rows


def project_kernel(back_ref, weight_ref, resid_ref, gain_ref, mixed_ref, normed_ref):
    rows = resid_ref.shape[0]
    attn = jnp.concatenate([back_ref[head, :rows, :] for head in range(back_ref.shape[0])], axis=1)
    mixed = resid_ref[...].astype(jnp.float32) + jnp.dot(
        attn, weight_ref[...], preferred_element_type=jnp.float32
    )
    mixed_ref[...] = mixed
    scale = lax.rsqrt(jnp.mean(mixed * mixed, axis=1, keepdims=True) + EPSILON)
    normed_ref[...] = (mixed * scale * gain_ref[...]).astype(jnp.bfloat16)


def mixture_kernel(
    at_ref,
    first_ref,
    second_ref,
    back_ref,
    router_ref,
    up_a,
    up_b,
    in_a,
    in_b,
    down_a,
    down_b,
    out_a,
    out_b,
    first_out,
    second_out,
):
    rows, width = first_ref.shape
    own = at_ref[0].astype(jnp.float32)

    def is_own(shard):
        ids = back_ref[shard, rows : rows + 16, :].astype(jnp.float32)[0:1, :]
        return (jnp.transpose(jnp.broadcast_to(ids, (rows, rows)))[:, 0:1] == own).astype(jnp.float32)

    normed = jnp.concatenate([first_ref[...], second_ref[...]], axis=0)
    mine = jnp.concatenate([is_own(at_ref[1]), is_own(at_ref[2])], axis=0)
    column = jnp.where(mine > 0, router_ref[0:1, :], router_ref[1:2, :])
    logits = jnp.sum(normed.astype(jnp.float32) * column, axis=1, keepdims=True)
    gate = jax.nn.sigmoid(logits)

    def hidden(weights):
        return jax.nn.gelu(jnp.dot(normed, weights[...], preferred_element_type=jnp.float32))

    mlp_a = hidden(up_a).astype(jnp.bfloat16)
    mlp_b = hidden(up_b).astype(jnp.bfloat16)
    exp_a = jnp.where(mine > 0, hidden(in_a), 0.0).astype(jnp.bfloat16)
    exp_b = jnp.where(mine > 0, 0.0, hidden(in_b)).astype(jnp.bfloat16)
    contract = (((1,), (1,)), ((), ()))
    step = min(width, 512)
    for begin in range(0, width, step):
        span = slice(begin, begin + step)
        part = gate * (
            jnp.dot(exp_a, out_a[:, span], preferred_element_type=jnp.float32)
            + jnp.dot(exp_b, out_b[:, span], preferred_element_type=jnp.float32)
        )
        part = part + (
            lax.dot_general(mlp_a, down_a[span, :], contract, preferred_element_type=jnp.float32)
            + lax.dot_general(mlp_b, down_b[span, :], contract, preferred_element_type=jnp.float32)
        )
        part = part.astype(jnp.bfloat16)
        first_out[:, span] = part[:rows]
        second_out[:, span] = part[rows:]


def body_by_pairs(
    queries,
    keys,
    values,
    resid,
    out_proj,
    norm_gain,
    up_proj,
    down_proj,
    router,
    expert_ids,
    expert_in,
    expert_out,
):
    rows, width = resid.shape
    heads = queries.shape[1] // DH
    ctx_count = lax.axis_size("ctx")
    device_index = lax.axis_index("ctx")
    core = device_index % 2
    exchange = functools.partial(
        lax.all_to_all,
        axis_name="ctx",
        split_axis=0,
        concat_axis=0,
        tiled=True,
        axis_index_groups=[list(range(parity, ctx_count, 2)) for parity in range(2)],
    )
    shape = jax.ShapeDtypeStruct
    (packed,) = call(
        pack_kernel,
        [shape((heads, rows, 3 * DH), jnp.bfloat16)],
        [VMEM] * 3,
        0,
        8,
        queries,
        keys,
        values,
    )
    own = exchange(packed)
    other = swap(own, 1)
    weights_own = (up_proj, expert_in[0], down_proj, expert_out[0])
    weights_other = tuple(swap(array, 1) for array in weights_own)
    weights = tuple(w for pair in zip(weights_own, weights_other) for w in pair)
    (out,) = call(
        attention_kernel,
        [shape((heads, rows + 16, DH), jnp.bfloat16)],
        [SMEM] + [VMEM] * 3,
        10**9,
        12,
        core.reshape(1),
        own,
        other,
        expert_ids.reshape(1, rows),
    )
    back = exchange(out)
    mixed, normed = call(
        project_kernel,
        [shape((rows, width), jnp.float32), shape((rows, width), jnp.bfloat16)],
        [VMEM] * 4,
        2 * out_proj.size * rows,
        12,
        back,
        out_proj,
        resid,
        norm_gain.reshape(1, width),
    )
    router_rows = router.astype(jnp.float32).T
    router_rows = jnp.where(core == 0, router_rows, router_rows[::-1])
    units = sum(w.size for w in weights[:4]) // width

    far_first = [4 * at for at in range(ctx_count // 4 - 1, 0, -1)]
    near = {0: normed}
    for offset in far_first:
        near[offset] = swap(normed, offset)
    across = {offset: swap(near[offset], 2) for offset in [0] + far_first}
    total = mixed
    for offset in far_first + [0]:
        places = [core] + [(device_index ^ mask) // 2 for mask in (offset, offset | 2)]
        part, part_across = call(
            mixture_kernel,
            [shape((rows, width), jnp.bfloat16)] * 2,
            [SMEM] + [VMEM] * 12,
            8 * rows * width * units,
            16,
            jnp.stack(places),
            near[offset],
            across[offset],
            back,
            router_rows,
            *weights,
        )
        summed = part.astype(jnp.float32) + swap(part_across, 2).astype(jnp.float32)
        if offset:
            summed = swap(summed.astype(jnp.bfloat16), offset).astype(jnp.float32)
        total = total + summed
    return total.astype(jnp.bfloat16)


def solution(mesh):
    ctx_count = mesh.shape["ctx"]

    def by_pairs(args):
        queries, router = args[0], args[8]
        return (
            router.shape[1] == 2
            and ctx_count == 2 * SPLIT
            and queries.shape[1] == ctx_count // 2 * DH
            and ctx_count % 4 == 0
            and ctx_count & (ctx_count - 1) == 0
        )

    def chosen(*args):
        if not by_pairs(args):
            return body(*args)
        return body_by_pairs(*args)

    placed = (
        P(("groups", "ctx"), None),
        P(("groups", "ctx"), None),
        P(("groups", "ctx"), None),
        P(("groups", "ctx"), None),
        P(),
        P(),
        P(None, "ctx"),
        P(None, "ctx"),
        P(),
        P(("groups", "ctx"), None),
        P("ctx", None, None),
        P("ctx", None, None),
    )
    return jax.shard_map(
        chosen, mesh=mesh, in_specs=placed, out_specs=P(("groups", "ctx"), None), check_vma=False
    )
```

```python
import functools
import jax
import jax.numpy as jnp
from jax import lax
from jax.experimental import pallas as pl
from jax.experimental.pallas import tpu as pltpu
from jax.sharding import PartitionSpec as P

DH = 128
SPLIT = 8


NEG_FILL = -1e30
EPSILON = 1e-06


def from_partner(array, axis, apart):
    return lax.ppermute(array, axis, [(i, i ^ 1 << apart) for i in range(lax.axis_size(axis))])


def update_state(state, query_rows, query_offset, key_block, value_block, key_offset):
    maxima, totals, numer = state
    count_query = query_rows.shape[0]
    count_keys = key_block.shape[0]
    head_count = query_rows.shape[1] // DH
    query_heads = query_rows.reshape(count_query, head_count, DH)
    key_heads = key_block.reshape(count_keys, head_count, DH)
    value_heads = value_block.reshape(count_keys, head_count, DH)
    scores = jnp.einsum(
        "qhd,khd->hqk", query_heads, key_heads, preferred_element_type=jnp.float32
    ) * DH ** (-0.5)
    query_positions = query_offset + jnp.arange(count_query, dtype=jnp.int32)
    key_positions = key_offset + jnp.arange(count_keys, dtype=jnp.int32)
    visible = (key_positions[None, :] <= query_positions[:, None])[None]
    masked = jnp.where(visible, scores, NEG_FILL)
    new_max = jnp.maximum(maxima, jnp.max(masked, axis=2))
    weights = jnp.where(visible, jnp.exp(masked - new_max[..., None]), 0.0)
    factor = jnp.exp(maxima - new_max)
    totals = totals * factor + jnp.sum(weights, axis=2)
    numer = numer * factor[..., None] + jnp.einsum(
        "hqk,khd->hqd",
        weights.astype(jnp.bfloat16),
        value_heads,
        preferred_element_type=jnp.float32,
    )
    return (new_max, totals, numer)


def attend(query_sets, keys, values):
    head_count = keys.shape[1] // DH
    initial = []
    for query_rows, query_offset in query_sets:
        count_query = query_rows.shape[0]
        initial.append(
            (
                jnp.full((head_count, count_query), NEG_FILL, jnp.float32),
                jnp.zeros((head_count, count_query), jnp.float32),
                jnp.zeros((head_count, count_query, DH), jnp.float32),
            )
        )
    states = tuple(initial)
    key_offset = jnp.int32(0)
    key_whole = lax.all_gather(keys, "ctx", axis=0, tiled=True)
    value_whole = lax.all_gather(values, "ctx", axis=0, tiled=True)
    total_keys = key_whole.shape[0]
    step_rows = min(total_keys, 1024)
    for begin in range(0, total_keys, step_rows):
        key_block = key_whole[begin : begin + step_rows]
        value_block = value_whole[begin : begin + step_rows]
        block_offset = key_offset + begin
        query_rows, query_offset = query_sets[0]
        needed = block_offset <= query_offset + query_rows.shape[0] - 1
        updated = [
            lax.cond(
                needed,
                lambda carried, rows_now=query_rows, offset_now=query_offset, keys_now=key_block, values_now=value_block, start_now=block_offset: update_state(
                    carried, rows_now, offset_now, keys_now, values_now, start_now
                ),
                lambda carried: carried,
                states[0],
            )
        ]
        states = tuple(updated)
    results = []
    for maxima, totals, numer in states:
        result = (numer / totals[..., None]).astype(jnp.bfloat16)
        results.append(
            jnp.transpose(result, (1, 0, 2)).reshape(result.shape[1], result.shape[0] * DH)
        )
    return results


def body(
    queries,
    keys,
    values,
    resid,
    out_proj,
    norm_gain,
    up_proj,
    down_proj,
    router,
    expert_ids,
    expert_in,
    expert_out,
):
    tok_rows = queries.shape[0]
    width = resid.shape[1]
    live_count = router.shape[1]
    ctx_count = lax.axis_size("ctx")
    device_index = lax.axis_index("ctx")
    base_offset = device_index * tok_rows
    attn = attend([(queries, base_offset)], keys, values)[0]
    mixed = resid.astype(jnp.float32) + jnp.dot(attn, out_proj, preferred_element_type=jnp.float32)
    normed = (
        mixed * lax.rsqrt(jnp.mean(mixed * mixed, axis=1, keepdims=True) + EPSILON) * norm_gain
    ).astype(jnp.bfloat16)
    mlp_blocks = jnp.stack([up_proj, down_proj], 0)
    for level in range(live_count.bit_length() - 1):
        other_block = from_partner(mlp_blocks, "ctx", level)
        mlp_blocks = jnp.concatenate([mlp_blocks, other_block], axis=2)
    slots_per = max(2, 5 * tok_rows // (4 * live_count))
    chosen = expert_ids[:, 0]
    onehot = (chosen[:, None] == jnp.arange(live_count, dtype=jnp.int32)[None, :]).astype(
        jnp.bfloat16
    )
    row_iota = jnp.arange(tok_rows, dtype=jnp.int32)
    strictly_lower = (row_iota[None, :] < row_iota[:, None]).astype(jnp.bfloat16)
    counts_before = jnp.dot(strictly_lower, onehot, preferred_element_type=jnp.float32)
    slot_index = jnp.sum(onehot.astype(jnp.float32) * counts_before, axis=1).astype(jnp.int32)
    target_slot = chosen * slots_per + slot_index
    dispatch_matrix = (
        jnp.arange(live_count * slots_per, dtype=jnp.int32)[:, None] == target_slot[None, :]
    ).astype(jnp.bfloat16)
    packed = jnp.dot(dispatch_matrix, normed, preferred_element_type=jnp.float32).astype(
        jnp.bfloat16
    )
    sending = jnp.broadcast_to(
        packed.reshape(1, live_count, slots_per, width), (SPLIT, live_count, slots_per, width)
    )
    sending = sending.reshape(ctx_count, 1, slots_per, width)
    own_expert = device_index % live_count
    router_column = lax.dynamic_slice_in_dim(router, own_expert, 1, 1)
    weight_in = expert_in[0]
    weight_out = expert_out[0]
    received = lax.all_to_all(sending, "ctx", split_axis=0, concat_axis=1, tiled=True)
    rows = received.reshape(-1, width)
    expert_hidden = jax.nn.gelu(
        jnp.dot(rows, weight_in, preferred_element_type=jnp.float32)
    ).astype(jnp.bfloat16)
    mlp_hidden = jax.nn.gelu(
        jnp.dot(rows, mlp_blocks[0], preferred_element_type=jnp.float32)
    ).astype(jnp.bfloat16)
    gate = jax.nn.sigmoid(jnp.dot(rows, router_column, preferred_element_type=jnp.float32))
    produced = gate * jnp.dot(expert_hidden, weight_out, preferred_element_type=jnp.float32)
    produced = produced + lax.dot_general(
        mlp_hidden, mlp_blocks[1], (((1,), (1,)), ((), ())), preferred_element_type=jnp.float32
    )
    came_back = lax.all_to_all(
        produced.astype(jnp.bfloat16).reshape(received.shape),
        "ctx",
        split_axis=1,
        concat_axis=0,
        tiled=True,
    )
    summed = jnp.sum(
        came_back.astype(jnp.float32).reshape(SPLIT, live_count * slots_per, width), axis=0
    )
    mixture_part = lax.dot_general(
        dispatch_matrix.astype(jnp.float32),
        summed,
        (((0,), (0,)), ((), ())),
        precision=lax.Precision.HIGHEST,
        preferred_element_type=jnp.float32,
    )
    return (mixed + mixture_part).astype(jnp.bfloat16)


def swap(array, mask):
    return lax.ppermute(array, "ctx", [(i, i ^ mask) for i in range(lax.axis_size("ctx"))])


VMEM = pl.BlockSpec(memory_space=pltpu.VMEM)
SMEM = pl.BlockSpec(memory_space=pltpu.SMEM)


HBM = pl.BlockSpec(memory_space=pltpu.HBM)


def call(kernel, outs, specs, flops, mib, *operands, copies=0, scratch=()):
    return pl.pallas_call(
        kernel,
        out_shape=outs,
        in_specs=specs,
        out_specs=[VMEM] * len(outs),
        scratch_shapes=[*scratch] + ([pltpu.SemaphoreType.DMA((copies,))] if copies else []),
        compiler_params=pltpu.CompilerParams(vmem_limit_bytes=mib * 2**20),
        cost_estimate=pl.CostEstimate(
            flops=flops,
            bytes_accessed=sum(x.size * x.dtype.itemsize for x in operands),
            transcendentals=0,
        ),
    )(*operands)


def copy_all(pairs, sems):
    copies = [pltpu.make_async_copy(a, b, sems.at[at]) for at, (a, b) in enumerate(pairs)]
    for copy in copies:
        copy.start()
    for copy in copies:
        copy.wait()


def load_kernel(*refs):
    count = len(refs) // 2
    copy_all(zip(refs[:count], refs[count : 2 * count]), refs[-1])


def load(*arrays):
    outs = [pltpu.VMEM(array.shape, array.dtype) for array in arrays]
    count = len(arrays)
    return call(load_kernel, outs, [HBM] * count, 0, 36, *arrays, copies=count)


def pack_kernel(query_ref, key_ref, value_ref, out_ref, sems):
    copy_all(
        [
            (ref.at[:, pl.ds(head * DH, DH)], out_ref.at[head, :, pl.ds(at * DH, DH)])
            for at, ref in enumerate((query_ref, key_ref, value_ref))
            for head in range(out_ref.shape[0])
        ],
        sems,
    )


def attention_kernel(index_ref, own_ref, other_ref, ids_ref, out_ref):
    core = index_ref[0] & 1
    blocks, rows, _ = own_ref.shape
    row_at = lax.broadcasted_iota(jnp.int32, (rows, rows), 0)
    column_at = lax.broadcasted_iota(jnp.int32, (rows, rows), 1)
    causal = column_at <= row_at
    also = jnp.broadcast_to(core == 1, (rows, rows))
    contract = (((1,), (1,)), ((), ()))
    id_rows = jnp.broadcast_to(
        ids_ref[...].astype(jnp.float32), (out_ref.shape[1] - rows, rows)
    ).astype(jnp.bfloat16)
    for block in range(blocks):
        query = own_ref[block, :, :DH]
        scores = []
        for ref, last_visible in ((own_ref, causal), (other_ref, also)):
            for at in range(block + 1):
                score = lax.dot_general(
                    query,
                    ref[at, :, DH : 2 * DH],
                    contract,
                    preferred_element_type=jnp.float32,
                ) * DH ** (-0.5)
                if at == block:
                    score = jnp.where(last_visible, score, NEG_FILL)
                scores.append(score)
        peak = scores[0]
        for score in scores[1:]:
            peak = jnp.maximum(peak, score)
        row_max = jnp.max(peak, axis=1, keepdims=True)
        numer = jnp.zeros((rows, DH), jnp.float32)
        summed = jnp.zeros((rows, rows), jnp.float32)
        for at, score in enumerate(scores):
            weights = jnp.exp(score - row_max)
            summed = summed + weights
            ref = own_ref if at <= block else other_ref
            numer = numer + jnp.dot(
                weights.astype(jnp.bfloat16),
                ref[at % (block + 1), :, 2 * DH :],
                preferred_element_type=jnp.float32,
            )
        totals = jnp.sum(summed, axis=1, keepdims=True)
        out_ref[block, :rows, :] = (numer / totals).astype(jnp.bfloat16)
        out_ref[block, rows:, :] = id_rows


def project_kernel(back_ref, weight_ref, resid_ref, gain_ref, mixed_ref, normed_ref, held, resid, sems):
    rows = resid_ref.shape[0]
    pieces = held.shape[0]
    depth = held.shape[1]
    copies = [
        pltpu.make_async_copy(weight_ref.at[pl.ds(at * depth, depth), :], held.at[at], sems.at[at])
        for at in range(pieces)
    ]
    copies.append(pltpu.make_async_copy(resid_ref, resid, sems.at[pieces]))
    for copy in copies[-1:] + copies[:-1]:
        copy.start()
    attn = jnp.concatenate([back_ref[head, :rows, :] for head in range(back_ref.shape[0])], axis=1)
    copies[-1].wait()
    mixed = resid[...].astype(jnp.float32)
    for at in range(pieces):
        copies[at].wait()
        mixed = mixed + jnp.dot(
            attn[:, at * depth : (at + 1) * depth], held[at], preferred_element_type=jnp.float32
        )
    mixed_ref[...] = mixed
    scale = lax.rsqrt(jnp.mean(mixed * mixed, axis=1, keepdims=True) + EPSILON)
    normed_ref[...] = (mixed * scale * gain_ref[...]).astype(jnp.bfloat16)


def mixture_kernel(
    offset,
    index_ref,
    first_ref,
    second_ref,
    back_ref,
    router_ref,
    up_a,
    up_b,
    in_a,
    in_b,
    down_a,
    down_b,
    out_a,
    out_b,
    first_out,
    second_out,
):
    rows, width = first_ref.shape
    own = (index_ref[0] & 1).astype(jnp.float32)

    def expert(mask):
        ids = back_ref[(index_ref[0] ^ mask) >> 1, rows : rows + 16, :].astype(jnp.float32)[0:1, :]
        return jnp.transpose(jnp.broadcast_to(ids, (rows, rows)))[:, 0:1]

    normed = jnp.concatenate([first_ref[...], second_ref[...]], axis=0)
    chosen = jnp.concatenate([expert(offset), expert(offset | 2)], axis=0)
    mine = chosen == own
    router = router_ref[...].astype(jnp.float32)
    column = jnp.where(chosen > 0, router[1:2, :], router[0:1, :])
    logits = jnp.sum(normed.astype(jnp.float32) * column, axis=1, keepdims=True)
    gate = jax.nn.sigmoid(logits)

    def hidden(weights):
        return jax.nn.gelu(jnp.dot(normed, weights[...], preferred_element_type=jnp.float32))

    mlp_a = hidden(up_a).astype(jnp.bfloat16)
    mlp_b = hidden(up_b).astype(jnp.bfloat16)
    exp_a = jnp.where(mine, hidden(in_a), 0.0).astype(jnp.bfloat16)
    exp_b = jnp.where(mine, 0.0, hidden(in_b)).astype(jnp.bfloat16)
    contract = (((1,), (1,)), ((), ()))
    step = min(width, 512)
    for begin in range(0, width, step):
        span = slice(begin, begin + step)
        part = gate * (
            jnp.dot(exp_a, out_a[:, span], preferred_element_type=jnp.float32)
            + jnp.dot(exp_b, out_b[:, span], preferred_element_type=jnp.float32)
        )
        part = part + (
            lax.dot_general(mlp_a, down_a[span, :], contract, preferred_element_type=jnp.float32)
            + lax.dot_general(mlp_b, down_b[span, :], contract, preferred_element_type=jnp.float32)
        )
        part = part.astype(jnp.bfloat16)
        first_out[:, span] = part[:rows]
        second_out[:, span] = part[rows:]


def body_by_pairs(
    queries,
    keys,
    values,
    resid,
    out_proj,
    norm_gain,
    up_proj,
    down_proj,
    router,
    expert_ids,
    expert_in,
    expert_out,
):
    rows, width = resid.shape
    heads = queries.shape[1] // DH
    ctx_count = lax.axis_size("ctx")
    device_index = lax.axis_index("ctx")
    index = device_index.reshape(1)
    exchange = functools.partial(
        lax.all_to_all,
        axis_name="ctx",
        split_axis=0,
        concat_axis=0,
        tiled=True,
        axis_index_groups=[list(range(parity, ctx_count, 2)) for parity in range(2)],
    )
    shape = jax.ShapeDtypeStruct
    (packed,) = call(
        pack_kernel,
        [shape((heads, rows, 3 * DH), jnp.bfloat16)],
        [HBM] * 3,
        0,
        62,
        queries,
        keys,
        values,
        copies=3 * heads,
    )
    own = exchange(packed)
    other = swap(own, 1)
    weights_own = (up_proj, expert_in[0], down_proj, expert_out[0])
    weights_other = [swap(array, 1) for array in weights_own]
    weights_own = load(*weights_own)
    weights_other = load(*weights_other)
    weights = tuple(w for pair in zip(weights_own, weights_other) for w in pair)
    (out,) = call(
        attention_kernel,
        [shape((heads, rows + 16, DH), jnp.bfloat16)],
        [SMEM] + [VMEM] * 3,
        10**9,
        12,
        index,
        own,
        other,
        expert_ids.reshape(1, rows),
    )
    back = exchange(out)
    pieces = heads // 2
    mixed, normed = call(
        project_kernel,
        [pltpu.VMEM((rows, width), jnp.float32), shape((rows, width), jnp.bfloat16)],
        [VMEM, HBM, HBM, VMEM],
        2 * out_proj.size * rows,
        58,
        back,
        out_proj,
        resid,
        norm_gain.reshape(1, width),
        copies=pieces + 1,
        scratch=[
            pltpu.VMEM((pieces, out_proj.shape[0] // pieces, width), out_proj.dtype),
            pltpu.VMEM(resid.shape, resid.dtype),
        ],
    )
    units = sum(w.size for w in weights[:4]) // width

    def mix(offset, first, second):
        return call(
            functools.partial(mixture_kernel, offset),
            [pltpu.VMEM((rows, width), jnp.bfloat16)] * 2,
            [SMEM] + [VMEM] * 12,
            8 * rows * width * units,
            16,
            index,
            first,
            second,
            back,
            router.T,
            *weights,
        )

    def plus(first, second):
        return first.astype(jnp.float32) + second.astype(jnp.float32)

    far = [4 * at for at in range(ctx_count // 4 - 1, 1, -1)]
    gathered = {offset: swap(normed, offset) for offset in far}
    across = swap(normed, 2)
    beside = swap(normed, 4)
    beside_across = swap(across, 4)
    total = mixed
    for offset in far:
        first = gathered[offset]
        part, part_across = mix(offset, first, swap(first, 2))
        summed = plus(part, swap(part_across, 2)).astype(jnp.bfloat16)
        total = total + swap(summed, offset).astype(jnp.float32)
    part, part_across = mix(0, normed, across)
    part_beside, part_both = mix(4, beside, beside_across)
    summed = plus(part_across, swap(part_both, 4)).astype(jnp.bfloat16)
    total = total + plus(part, swap(part_beside, 4))
    total = total + swap(summed, 2).astype(jnp.float32)
    return total.astype(jnp.bfloat16)


def solution(mesh):
    ctx_count = mesh.shape["ctx"]

    def by_pairs(args):
        queries, router = args[0], args[8]
        return (
            router.shape[1] == 2
            and ctx_count == 2 * SPLIT
            and queries.shape[1] == ctx_count // 2 * DH
            and ctx_count % 4 == 0
            and ctx_count & (ctx_count - 1) == 0
        )

    def chosen(*args):
        if not by_pairs(args):
            return body(*args)
        return body_by_pairs(*args)

    placed = (
        P(("groups", "ctx"), None),
        P(("groups", "ctx"), None),
        P(("groups", "ctx"), None),
        P(("groups", "ctx"), None),
        P(),
        P(),
        P(None, "ctx"),
        P(None, "ctx"),
        P(),
        P(("groups", "ctx"), None),
        P("ctx", None, None),
        P("ctx", None, None),
    )
    return jax.shard_map(
        chosen, mesh=mesh, in_specs=placed, out_specs=P(("groups", "ctx"), None), check_vma=False
    )
```

```python
import functools
import jax
import jax.numpy as jnp
from jax import lax
from jax.experimental import pallas as pl
from jax.experimental.pallas import tpu as pltpu
from jax.sharding import PartitionSpec as P

DH = 128
SPLIT = 8


NEG_FILL = -1e30
EPSILON = 1e-06


def from_partner(array, axis, apart):
    return lax.ppermute(array, axis, [(i, i ^ 1 << apart) for i in range(lax.axis_size(axis))])


def update_state(state, query_rows, query_offset, key_block, value_block, key_offset):
    maxima, totals, numer = state
    count_query = query_rows.shape[0]
    count_keys = key_block.shape[0]
    head_count = query_rows.shape[1] // DH
    query_heads = query_rows.reshape(count_query, head_count, DH)
    key_heads = key_block.reshape(count_keys, head_count, DH)
    value_heads = value_block.reshape(count_keys, head_count, DH)
    scores = jnp.einsum(
        "qhd,khd->hqk", query_heads, key_heads, preferred_element_type=jnp.float32
    ) * DH ** (-0.5)
    query_positions = query_offset + jnp.arange(count_query, dtype=jnp.int32)
    key_positions = key_offset + jnp.arange(count_keys, dtype=jnp.int32)
    visible = (key_positions[None, :] <= query_positions[:, None])[None]
    masked = jnp.where(visible, scores, NEG_FILL)
    new_max = jnp.maximum(maxima, jnp.max(masked, axis=2))
    weights = jnp.where(visible, jnp.exp(masked - new_max[..., None]), 0.0)
    factor = jnp.exp(maxima - new_max)
    totals = totals * factor + jnp.sum(weights, axis=2)
    numer = numer * factor[..., None] + jnp.einsum(
        "hqk,khd->hqd",
        weights.astype(jnp.bfloat16),
        value_heads,
        preferred_element_type=jnp.float32,
    )
    return (new_max, totals, numer)


def attend(query_sets, keys, values):
    head_count = keys.shape[1] // DH
    initial = []
    for query_rows, query_offset in query_sets:
        count_query = query_rows.shape[0]
        initial.append(
            (
                jnp.full((head_count, count_query), NEG_FILL, jnp.float32),
                jnp.zeros((head_count, count_query), jnp.float32),
                jnp.zeros((head_count, count_query, DH), jnp.float32),
            )
        )
    states = tuple(initial)
    key_offset = jnp.int32(0)
    key_whole = lax.all_gather(keys, "ctx", axis=0, tiled=True)
    value_whole = lax.all_gather(values, "ctx", axis=0, tiled=True)
    total_keys = key_whole.shape[0]
    step_rows = min(total_keys, 1024)
    for begin in range(0, total_keys, step_rows):
        key_block = key_whole[begin : begin + step_rows]
        value_block = value_whole[begin : begin + step_rows]
        block_offset = key_offset + begin
        query_rows, query_offset = query_sets[0]
        needed = block_offset <= query_offset + query_rows.shape[0] - 1
        updated = [
            lax.cond(
                needed,
                lambda carried, rows_now=query_rows, offset_now=query_offset, keys_now=key_block, values_now=value_block, start_now=block_offset: update_state(
                    carried, rows_now, offset_now, keys_now, values_now, start_now
                ),
                lambda carried: carried,
                states[0],
            )
        ]
        states = tuple(updated)
    results = []
    for maxima, totals, numer in states:
        result = (numer / totals[..., None]).astype(jnp.bfloat16)
        results.append(
            jnp.transpose(result, (1, 0, 2)).reshape(result.shape[1], result.shape[0] * DH)
        )
    return results


def body(
    queries,
    keys,
    values,
    resid,
    out_proj,
    norm_gain,
    up_proj,
    down_proj,
    router,
    expert_ids,
    expert_in,
    expert_out,
):
    tok_rows = queries.shape[0]
    width = resid.shape[1]
    live_count = router.shape[1]
    ctx_count = lax.axis_size("ctx")
    device_index = lax.axis_index("ctx")
    base_offset = device_index * tok_rows
    attn = attend([(queries, base_offset)], keys, values)[0]
    mixed = resid.astype(jnp.float32) + jnp.dot(attn, out_proj, preferred_element_type=jnp.float32)
    normed = (
        mixed * lax.rsqrt(jnp.mean(mixed * mixed, axis=1, keepdims=True) + EPSILON) * norm_gain
    ).astype(jnp.bfloat16)
    mlp_blocks = jnp.stack([up_proj, down_proj], 0)
    for level in range(live_count.bit_length() - 1):
        other_block = from_partner(mlp_blocks, "ctx", level)
        mlp_blocks = jnp.concatenate([mlp_blocks, other_block], axis=2)
    slots_per = max(2, 5 * tok_rows // (4 * live_count))
    chosen = expert_ids[:, 0]
    onehot = (chosen[:, None] == jnp.arange(live_count, dtype=jnp.int32)[None, :]).astype(
        jnp.bfloat16
    )
    row_iota = jnp.arange(tok_rows, dtype=jnp.int32)
    strictly_lower = (row_iota[None, :] < row_iota[:, None]).astype(jnp.bfloat16)
    counts_before = jnp.dot(strictly_lower, onehot, preferred_element_type=jnp.float32)
    slot_index = jnp.sum(onehot.astype(jnp.float32) * counts_before, axis=1).astype(jnp.int32)
    target_slot = chosen * slots_per + slot_index
    dispatch_matrix = (
        jnp.arange(live_count * slots_per, dtype=jnp.int32)[:, None] == target_slot[None, :]
    ).astype(jnp.bfloat16)
    packed = jnp.dot(dispatch_matrix, normed, preferred_element_type=jnp.float32).astype(
        jnp.bfloat16
    )
    sending = jnp.broadcast_to(
        packed.reshape(1, live_count, slots_per, width), (SPLIT, live_count, slots_per, width)
    )
    sending = sending.reshape(ctx_count, 1, slots_per, width)
    own_expert = device_index % live_count
    router_column = lax.dynamic_slice_in_dim(router, own_expert, 1, 1)
    weight_in = expert_in[0]
    weight_out = expert_out[0]
    received = lax.all_to_all(sending, "ctx", split_axis=0, concat_axis=1, tiled=True)
    rows = received.reshape(-1, width)
    expert_hidden = jax.nn.gelu(
        jnp.dot(rows, weight_in, preferred_element_type=jnp.float32)
    ).astype(jnp.bfloat16)
    mlp_hidden = jax.nn.gelu(
        jnp.dot(rows, mlp_blocks[0], preferred_element_type=jnp.float32)
    ).astype(jnp.bfloat16)
    gate = jax.nn.sigmoid(jnp.dot(rows, router_column, preferred_element_type=jnp.float32))
    produced = gate * jnp.dot(expert_hidden, weight_out, preferred_element_type=jnp.float32)
    produced = produced + lax.dot_general(
        mlp_hidden, mlp_blocks[1], (((1,), (1,)), ((), ())), preferred_element_type=jnp.float32
    )
    came_back = lax.all_to_all(
        produced.astype(jnp.bfloat16).reshape(received.shape),
        "ctx",
        split_axis=1,
        concat_axis=0,
        tiled=True,
    )
    summed = jnp.sum(
        came_back.astype(jnp.float32).reshape(SPLIT, live_count * slots_per, width), axis=0
    )
    mixture_part = lax.dot_general(
        dispatch_matrix.astype(jnp.float32),
        summed,
        (((0,), (0,)), ((), ())),
        precision=lax.Precision.HIGHEST,
        preferred_element_type=jnp.float32,
    )
    return (mixed + mixture_part).astype(jnp.bfloat16)


def swap(array, mask):
    return lax.ppermute(array, "ctx", [(i, i ^ mask) for i in range(lax.axis_size("ctx"))])


VMEM = pl.BlockSpec(memory_space=pltpu.VMEM)
SMEM = pl.BlockSpec(memory_space=pltpu.SMEM)


HBM = pl.BlockSpec(memory_space=pltpu.HBM)


def call(kernel, outs, specs, flops, mib, *operands, copies=0, scratch=()):
    return pl.pallas_call(
        kernel,
        out_shape=outs,
        in_specs=specs,
        out_specs=[VMEM] * len(outs),
        scratch_shapes=[*scratch] + ([pltpu.SemaphoreType.DMA((copies,))] if copies else []),
        compiler_params=pltpu.CompilerParams(vmem_limit_bytes=mib * 2**20),
        cost_estimate=pl.CostEstimate(
            flops=flops,
            bytes_accessed=sum(x.size * x.dtype.itemsize for x in operands),
            transcendentals=0,
        ),
    )(*operands)


def copy_all(pairs, sems):
    copies = [pltpu.make_async_copy(a, b, sems.at[at]) for at, (a, b) in enumerate(pairs)]
    for copy in copies:
        copy.start()
    for copy in copies:
        copy.wait()


def load_kernel(*refs):
    count = len(refs) // 2
    copy_all(zip(refs[:count], refs[count : 2 * count]), refs[-1])


def load(*arrays):
    outs = [pltpu.VMEM(array.shape, array.dtype) for array in arrays]
    count = len(arrays)
    return call(load_kernel, outs, [HBM] * count, 0, 36, *arrays, copies=count)


def pack_kernel(query_ref, key_ref, value_ref, out_ref, sems):
    copy_all(
        [
            (ref.at[:, pl.ds(head * DH, DH)], out_ref.at[head, :, pl.ds(at * DH, DH)])
            for at, ref in enumerate((query_ref, key_ref, value_ref))
            for head in range(out_ref.shape[0])
        ],
        sems,
    )


def attention_kernel(index_ref, own_ref, other_ref, ids_ref, out_ref):
    core = index_ref[0] & 1
    blocks, rows, _ = own_ref.shape
    row_at = lax.broadcasted_iota(jnp.int32, (rows, rows), 0)
    column_at = lax.broadcasted_iota(jnp.int32, (rows, rows), 1)
    causal = column_at <= row_at
    also = jnp.broadcast_to(core == 1, (rows, rows))
    contract = (((1,), (1,)), ((), ()))
    id_rows = jnp.broadcast_to(
        ids_ref[...].astype(jnp.float32), (out_ref.shape[1] - rows, rows)
    ).astype(jnp.bfloat16)
    for block in range(blocks):
        query = own_ref[block, :, :DH]
        scores = []
        for ref, last_visible in ((own_ref, causal), (other_ref, also)):
            for at in range(block + 1):
                score = lax.dot_general(
                    query,
                    ref[at, :, DH : 2 * DH],
                    contract,
                    preferred_element_type=jnp.float32,
                ) * DH ** (-0.5)
                if at == block:
                    score = jnp.where(last_visible, score, NEG_FILL)
                scores.append(score)
        peak = scores[0]
        for score in scores[1:]:
            peak = jnp.maximum(peak, score)
        row_max = jnp.max(peak, axis=1, keepdims=True)
        numer = jnp.zeros((rows, DH), jnp.float32)
        summed = jnp.zeros((rows, rows), jnp.float32)
        for at, score in enumerate(scores):
            weights = jnp.exp(score - row_max)
            summed = summed + weights
            ref = own_ref if at <= block else other_ref
            numer = numer + jnp.dot(
                weights.astype(jnp.bfloat16),
                ref[at % (block + 1), :, 2 * DH :],
                preferred_element_type=jnp.float32,
            )
        totals = jnp.sum(summed, axis=1, keepdims=True)
        out_ref[block, :rows, :] = (numer / totals).astype(jnp.bfloat16)
        out_ref[block, rows:, :] = id_rows


def project_kernel(
    back_ref, weight_ref, resid_ref, gain_ref, mixed_ref, normed_ref, held, back, resid, sems
):
    rows, width = resid_ref.shape
    pieces = held.shape[0]
    step = width // pieces
    copies = [
        pltpu.make_async_copy(back_ref, back, sems.at[pieces]),
        pltpu.make_async_copy(resid_ref, resid, sems.at[pieces + 1]),
    ] + [
        pltpu.make_async_copy(weight_ref.at[:, pl.ds(at * step, step)], held.at[at], sems.at[at])
        for at in range(pieces)
    ]
    for copy in copies:
        copy.start()
    copies[0].wait()
    attn = jnp.concatenate([back[head, :rows, :] for head in range(back.shape[0])], axis=1)
    copies[1].wait()
    squares = jnp.zeros((rows, 1), jnp.float32)
    for at in range(pieces):
        span = slice(at * step, (at + 1) * step)
        copies[at + 2].wait()
        mixed = resid[:, span].astype(jnp.float32) + jnp.dot(
            attn, held[at], preferred_element_type=jnp.float32
        )
        mixed_ref[:, span] = mixed
        squares = squares + jnp.sum(mixed * mixed, axis=1, keepdims=True)
    scale = lax.rsqrt(squares / width + EPSILON)
    normed_ref[...] = (mixed_ref[...] * scale * gain_ref[...]).astype(jnp.bfloat16)


def mixture_kernel(
    offset,
    index_ref,
    first_ref,
    second_ref,
    back_ref,
    router_ref,
    up_a,
    up_b,
    in_a,
    in_b,
    down_a,
    down_b,
    out_a,
    out_b,
    first_out,
    second_out,
):
    rows, width = first_ref.shape
    own = (index_ref[0] & 1).astype(jnp.float32)

    def expert(mask):
        ids = back_ref[(index_ref[0] ^ mask) >> 1, rows : rows + 16, :].astype(jnp.float32)[0:1, :]
        return jnp.transpose(jnp.broadcast_to(ids, (rows, rows)))[:, 0:1]

    normed = jnp.concatenate([first_ref[...], second_ref[...]], axis=0)
    chosen = jnp.concatenate([expert(offset), expert(offset | 2)], axis=0)
    mine = chosen == own
    router = router_ref[...].astype(jnp.float32)
    column = jnp.where(chosen > 0, router[1:2, :], router[0:1, :])
    logits = jnp.sum(normed.astype(jnp.float32) * column, axis=1, keepdims=True)
    gate = jax.nn.sigmoid(logits)

    def hidden(weights):
        return jax.nn.gelu(jnp.dot(normed, weights[...], preferred_element_type=jnp.float32))

    mlp_a = hidden(up_a).astype(jnp.bfloat16)
    mlp_b = hidden(up_b).astype(jnp.bfloat16)
    exp_a = jnp.where(mine, hidden(in_a), 0.0).astype(jnp.bfloat16)
    exp_b = jnp.where(mine, 0.0, hidden(in_b)).astype(jnp.bfloat16)
    contract = (((1,), (1,)), ((), ()))
    step = min(width, 512)
    for begin in range(0, width, step):
        span = slice(begin, begin + step)
        part = gate * (
            jnp.dot(exp_a, out_a[:, span], preferred_element_type=jnp.float32)
            + jnp.dot(exp_b, out_b[:, span], preferred_element_type=jnp.float32)
        )
        part = part + (
            lax.dot_general(mlp_a, down_a[span, :], contract, preferred_element_type=jnp.float32)
            + lax.dot_general(mlp_b, down_b[span, :], contract, preferred_element_type=jnp.float32)
        )
        part = part.astype(jnp.bfloat16)
        first_out[:, span] = part[:rows]
        second_out[:, span] = part[rows:]


def body_by_pairs(
    queries,
    keys,
    values,
    resid,
    out_proj,
    norm_gain,
    up_proj,
    down_proj,
    router,
    expert_ids,
    expert_in,
    expert_out,
):
    rows, width = resid.shape
    heads = queries.shape[1] // DH
    ctx_count = lax.axis_size("ctx")
    device_index = lax.axis_index("ctx")
    index = device_index.reshape(1)
    exchange = functools.partial(
        lax.all_to_all,
        axis_name="ctx",
        split_axis=0,
        concat_axis=0,
        tiled=True,
        axis_index_groups=[list(range(parity, ctx_count, 2)) for parity in range(2)],
    )
    shape = jax.ShapeDtypeStruct
    (packed,) = call(
        pack_kernel,
        [shape((heads, rows, 3 * DH), jnp.bfloat16)],
        [HBM] * 3,
        0,
        62,
        queries,
        keys,
        values,
        copies=3 * heads,
    )
    own = exchange(packed)
    other = swap(own, 1)
    weights_own = (up_proj, expert_in[0], down_proj, expert_out[0])
    weights_other = [swap(array, 1) for array in weights_own]
    weights_own = load(*weights_own)
    weights_other = load(*weights_other)
    weights = tuple(w for pair in zip(weights_own, weights_other) for w in pair)
    (out,) = call(
        attention_kernel,
        [shape((heads, rows + 16, DH), jnp.bfloat16)],
        [SMEM] + [VMEM] * 3,
        10**9,
        12,
        index,
        own,
        other,
        expert_ids.reshape(1, rows),
    )
    back = exchange(out)
    pieces = 4
    mixed, normed = call(
        project_kernel,
        [pltpu.VMEM((rows, width), jnp.float32), shape((rows, width), jnp.bfloat16)],
        [HBM, HBM, HBM, VMEM],
        2 * out_proj.size * rows,
        58,
        back,
        out_proj,
        resid,
        norm_gain.reshape(1, width),
        copies=pieces + 2,
        scratch=[
            pltpu.VMEM((pieces, out_proj.shape[0], width // pieces), out_proj.dtype),
            pltpu.VMEM(back.shape, back.dtype),
            pltpu.VMEM(resid.shape, resid.dtype),
        ],
    )
    units = sum(w.size for w in weights[:4]) // width

    def mix(offset, first, second):
        return call(
            functools.partial(mixture_kernel, offset),
            [pltpu.VMEM((rows, width), jnp.bfloat16)] * 2,
            [SMEM] + [VMEM] * 12,
            8 * rows * width * units,
            16,
            index,
            first,
            second,
            back,
            router.T,
            *weights,
        )

    def plus(first, second):
        return first.astype(jnp.float32) + second.astype(jnp.float32)

    far = [4 * at for at in range(ctx_count // 4 - 1, 1, -1)]
    gathered = {offset: swap(normed, offset) for offset in far}
    across = swap(normed, 2)
    beside = swap(normed, 4)
    beside_across = swap(across, 4)
    total = mixed
    for offset in far:
        first = gathered[offset]
        part, part_across = mix(offset, first, swap(first, 2))
        summed = plus(part, swap(part_across, 2)).astype(jnp.bfloat16)
        total = total + swap(summed, offset).astype(jnp.float32)
    part, part_across = mix(0, normed, across)
    part_beside, part_both = mix(4, beside, beside_across)
    summed = plus(part_across, swap(part_both, 4)).astype(jnp.bfloat16)
    total = total + plus(part, swap(part_beside, 4))
    total = total + swap(summed, 2).astype(jnp.float32)
    return total.astype(jnp.bfloat16)


def solution(mesh):
    ctx_count = mesh.shape["ctx"]

    def by_pairs(args):
        queries, router = args[0], args[8]
        return (
            router.shape[1] == 2
            and ctx_count == 2 * SPLIT
            and queries.shape[1] == ctx_count // 2 * DH
            and ctx_count % 4 == 0
            and ctx_count & (ctx_count - 1) == 0
        )

    def chosen(*args):
        if not by_pairs(args):
            return body(*args)
        return body_by_pairs(*args)

    placed = (
        P(("groups", "ctx"), None),
        P(("groups", "ctx"), None),
        P(("groups", "ctx"), None),
        P(("groups", "ctx"), None),
        P(),
        P(),
        P(None, "ctx"),
        P(None, "ctx"),
        P(),
        P(("groups", "ctx"), None),
        P("ctx", None, None),
        P("ctx", None, None),
    )
    return jax.shard_map(
        chosen, mesh=mesh, in_specs=placed, out_specs=P(("groups", "ctx"), None), check_vma=False
    )
```

```python
import functools
import jax
import jax.numpy as jnp
from jax import lax
from jax.experimental import pallas as pl
from jax.experimental.pallas import tpu as pltpu
from jax.sharding import PartitionSpec as P

DH = 128
SPLIT = 8


NEG_FILL = -1e30
EPSILON = 1e-06


def from_partner(array, axis, apart):
    return lax.ppermute(array, axis, [(i, i ^ 1 << apart) for i in range(lax.axis_size(axis))])


def update_state(state, query_rows, query_offset, key_block, value_block, key_offset):
    maxima, totals, numer = state
    count_query = query_rows.shape[0]
    count_keys = key_block.shape[0]
    head_count = query_rows.shape[1] // DH
    query_heads = query_rows.reshape(count_query, head_count, DH)
    key_heads = key_block.reshape(count_keys, head_count, DH)
    value_heads = value_block.reshape(count_keys, head_count, DH)
    scores = jnp.einsum(
        "qhd,khd->hqk", query_heads, key_heads, preferred_element_type=jnp.float32
    ) * DH ** (-0.5)
    query_positions = query_offset + jnp.arange(count_query, dtype=jnp.int32)
    key_positions = key_offset + jnp.arange(count_keys, dtype=jnp.int32)
    visible = (key_positions[None, :] <= query_positions[:, None])[None]
    masked = jnp.where(visible, scores, NEG_FILL)
    new_max = jnp.maximum(maxima, jnp.max(masked, axis=2))
    weights = jnp.where(visible, jnp.exp(masked - new_max[..., None]), 0.0)
    factor = jnp.exp(maxima - new_max)
    totals = totals * factor + jnp.sum(weights, axis=2)
    numer = numer * factor[..., None] + jnp.einsum(
        "hqk,khd->hqd",
        weights.astype(jnp.bfloat16),
        value_heads,
        preferred_element_type=jnp.float32,
    )
    return (new_max, totals, numer)


def attend(query_sets, keys, values):
    head_count = keys.shape[1] // DH
    initial = []
    for query_rows, query_offset in query_sets:
        count_query = query_rows.shape[0]
        initial.append(
            (
                jnp.full((head_count, count_query), NEG_FILL, jnp.float32),
                jnp.zeros((head_count, count_query), jnp.float32),
                jnp.zeros((head_count, count_query, DH), jnp.float32),
            )
        )
    states = tuple(initial)
    key_offset = jnp.int32(0)
    key_whole = lax.all_gather(keys, "ctx", axis=0, tiled=True)
    value_whole = lax.all_gather(values, "ctx", axis=0, tiled=True)
    total_keys = key_whole.shape[0]
    step_rows = min(total_keys, 1024)
    for begin in range(0, total_keys, step_rows):
        key_block = key_whole[begin : begin + step_rows]
        value_block = value_whole[begin : begin + step_rows]
        block_offset = key_offset + begin
        query_rows, query_offset = query_sets[0]
        needed = block_offset <= query_offset + query_rows.shape[0] - 1
        updated = [
            lax.cond(
                needed,
                lambda carried, rows_now=query_rows, offset_now=query_offset, keys_now=key_block, values_now=value_block, start_now=block_offset: update_state(
                    carried, rows_now, offset_now, keys_now, values_now, start_now
                ),
                lambda carried: carried,
                states[0],
            )
        ]
        states = tuple(updated)
    results = []
    for maxima, totals, numer in states:
        result = (numer / totals[..., None]).astype(jnp.bfloat16)
        results.append(
            jnp.transpose(result, (1, 0, 2)).reshape(result.shape[1], result.shape[0] * DH)
        )
    return results


def body(
    queries,
    keys,
    values,
    resid,
    out_proj,
    norm_gain,
    up_proj,
    down_proj,
    router,
    expert_ids,
    expert_in,
    expert_out,
):
    tok_rows = queries.shape[0]
    width = resid.shape[1]
    live_count = router.shape[1]
    ctx_count = lax.axis_size("ctx")
    device_index = lax.axis_index("ctx")
    base_offset = device_index * tok_rows
    attn = attend([(queries, base_offset)], keys, values)[0]
    mixed = resid.astype(jnp.float32) + jnp.dot(attn, out_proj, preferred_element_type=jnp.float32)
    normed = (
        mixed * lax.rsqrt(jnp.mean(mixed * mixed, axis=1, keepdims=True) + EPSILON) * norm_gain
    ).astype(jnp.bfloat16)
    mlp_blocks = jnp.stack([up_proj, down_proj], 0)
    for level in range(live_count.bit_length() - 1):
        other_block = from_partner(mlp_blocks, "ctx", level)
        mlp_blocks = jnp.concatenate([mlp_blocks, other_block], axis=2)
    slots_per = max(2, 5 * tok_rows // (4 * live_count))
    chosen = expert_ids[:, 0]
    onehot = (chosen[:, None] == jnp.arange(live_count, dtype=jnp.int32)[None, :]).astype(
        jnp.bfloat16
    )
    row_iota = jnp.arange(tok_rows, dtype=jnp.int32)
    strictly_lower = (row_iota[None, :] < row_iota[:, None]).astype(jnp.bfloat16)
    counts_before = jnp.dot(strictly_lower, onehot, preferred_element_type=jnp.float32)
    slot_index = jnp.sum(onehot.astype(jnp.float32) * counts_before, axis=1).astype(jnp.int32)
    target_slot = chosen * slots_per + slot_index
    dispatch_matrix = (
        jnp.arange(live_count * slots_per, dtype=jnp.int32)[:, None] == target_slot[None, :]
    ).astype(jnp.bfloat16)
    packed = jnp.dot(dispatch_matrix, normed, preferred_element_type=jnp.float32).astype(
        jnp.bfloat16
    )
    sending = jnp.broadcast_to(
        packed.reshape(1, live_count, slots_per, width), (SPLIT, live_count, slots_per, width)
    )
    sending = sending.reshape(ctx_count, 1, slots_per, width)
    own_expert = device_index % live_count
    router_column = lax.dynamic_slice_in_dim(router, own_expert, 1, 1)
    weight_in = expert_in[0]
    weight_out = expert_out[0]
    received = lax.all_to_all(sending, "ctx", split_axis=0, concat_axis=1, tiled=True)
    rows = received.reshape(-1, width)
    expert_hidden = jax.nn.gelu(
        jnp.dot(rows, weight_in, preferred_element_type=jnp.float32)
    ).astype(jnp.bfloat16)
    mlp_hidden = jax.nn.gelu(
        jnp.dot(rows, mlp_blocks[0], preferred_element_type=jnp.float32)
    ).astype(jnp.bfloat16)
    gate = jax.nn.sigmoid(jnp.dot(rows, router_column, preferred_element_type=jnp.float32))
    produced = gate * jnp.dot(expert_hidden, weight_out, preferred_element_type=jnp.float32)
    produced = produced + lax.dot_general(
        mlp_hidden, mlp_blocks[1], (((1,), (1,)), ((), ())), preferred_element_type=jnp.float32
    )
    came_back = lax.all_to_all(
        produced.astype(jnp.bfloat16).reshape(received.shape),
        "ctx",
        split_axis=1,
        concat_axis=0,
        tiled=True,
    )
    summed = jnp.sum(
        came_back.astype(jnp.float32).reshape(SPLIT, live_count * slots_per, width), axis=0
    )
    mixture_part = lax.dot_general(
        dispatch_matrix.astype(jnp.float32),
        summed,
        (((0,), (0,)), ((), ())),
        precision=lax.Precision.HIGHEST,
        preferred_element_type=jnp.float32,
    )
    return (mixed + mixture_part).astype(jnp.bfloat16)


def swap(array, mask):
    return lax.ppermute(array, "ctx", [(i, i ^ mask) for i in range(lax.axis_size("ctx"))])


VMEM = pl.BlockSpec(memory_space=pltpu.VMEM)
SMEM = pl.BlockSpec(memory_space=pltpu.SMEM)


HBM = pl.BlockSpec(memory_space=pltpu.HBM)


def call(kernel, outs, specs, flops, mib, *operands, copies=0, scratch=()):
    return pl.pallas_call(
        kernel,
        out_shape=outs,
        in_specs=specs,
        out_specs=[VMEM] * len(outs),
        scratch_shapes=[*scratch] + ([pltpu.SemaphoreType.DMA((copies,))] if copies else []),
        compiler_params=pltpu.CompilerParams(vmem_limit_bytes=mib * 2**20),
        cost_estimate=pl.CostEstimate(
            flops=flops,
            bytes_accessed=sum(x.size * x.dtype.itemsize for x in operands),
            transcendentals=0,
        ),
    )(*operands)


def copy_all(pairs, sems):
    copies = [pltpu.make_async_copy(a, b, sems.at[at]) for at, (a, b) in enumerate(pairs)]
    for copy in copies:
        copy.start()
    for copy in copies:
        copy.wait()


def load_kernel(*refs):
    count = len(refs) // 2
    copy_all(zip(refs[:count], refs[count : 2 * count]), refs[-1])


def load(mib, *arrays):
    outs = [pltpu.VMEM(array.shape, array.dtype) for array in arrays]
    count = len(arrays)
    return call(load_kernel, outs, [HBM] * count, 0, mib, *arrays, copies=count)


def pack_kernel(index_ref, query_ref, key_ref, value_ref, *refs):
    pairs = []
    for at, out_ref in enumerate(refs[:-1]):
        head = (index_ref[0] ^ 2 * at) >> 1
        columns = pl.ds(pl.multiple_of(head * DH, DH), DH)
        for part, ref in enumerate((query_ref, key_ref, value_ref)):
            pairs.append((ref.at[:, columns], out_ref.at[:, pl.ds(part * DH, DH)]))
    copy_all(pairs, refs[-1])


def arrange_kernel(index_ref, *refs):
    query_ref, pair_ref = refs[-2:]
    for at, ref in enumerate(refs[:-2]):
        place = (index_ref[0] ^ 2 * at) >> 1
        query_ref[place] = ref[:, :DH]
        pair_ref[place] = ref[:, DH:]


def attention_kernel(index_ref, query_ref, own_ref, other_ref, ids_ref, out_ref):
    core = index_ref[0] & 1
    blocks, rows, _ = own_ref.shape
    row_at = lax.broadcasted_iota(jnp.int32, (rows, rows), 0)
    column_at = lax.broadcasted_iota(jnp.int32, (rows, rows), 1)
    causal = column_at <= row_at
    also = jnp.broadcast_to(core == 1, (rows, rows))
    contract = (((1,), (1,)), ((), ()))
    id_rows = jnp.broadcast_to(
        ids_ref[...].astype(jnp.float32), (out_ref.shape[1] - rows, rows)
    ).astype(jnp.bfloat16)
    for block in range(blocks):
        query = query_ref[block]
        scores = []
        for ref, last_visible in ((own_ref, causal), (other_ref, also)):
            for at in range(block + 1):
                score = lax.dot_general(
                    query,
                    ref[at, :, :DH],
                    contract,
                    preferred_element_type=jnp.float32,
                ) * DH ** (-0.5)
                if at == block:
                    score = jnp.where(last_visible, score, NEG_FILL)
                scores.append(score)
        peak = scores[0]
        for score in scores[1:]:
            peak = jnp.maximum(peak, score)
        row_max = jnp.max(peak, axis=1, keepdims=True)
        numer = jnp.zeros((rows, DH), jnp.float32)
        summed = jnp.zeros((rows, rows), jnp.float32)
        for at, score in enumerate(scores):
            weights = jnp.exp(score - row_max)
            summed = summed + weights
            ref = own_ref if at <= block else other_ref
            numer = numer + jnp.dot(
                weights.astype(jnp.bfloat16),
                ref[at % (block + 1), :, DH:],
                preferred_element_type=jnp.float32,
            )
        totals = jnp.sum(summed, axis=1, keepdims=True)
        out_ref[block, :rows, :] = (numer / totals).astype(jnp.bfloat16)
        out_ref[block, rows:, :] = id_rows


def project_kernel(
    back_ref, weight_ref, resid_ref, gain_ref, mixed_ref, normed_ref, held, back, resid, sems
):
    rows, width = resid_ref.shape
    pieces = held.shape[0]
    step = width // pieces
    copies = [
        pltpu.make_async_copy(back_ref, back, sems.at[pieces]),
        pltpu.make_async_copy(resid_ref, resid, sems.at[pieces + 1]),
    ] + [
        pltpu.make_async_copy(weight_ref.at[:, pl.ds(at * step, step)], held.at[at], sems.at[at])
        for at in range(pieces)
    ]
    for copy in copies:
        copy.start()
    copies[0].wait()
    attn = jnp.concatenate([back[head, :rows, :] for head in range(back.shape[0])], axis=1)
    copies[1].wait()
    squares = jnp.zeros((rows, 1), jnp.float32)
    for at in range(pieces):
        span = slice(at * step, (at + 1) * step)
        copies[at + 2].wait()
        mixed = resid[:, span].astype(jnp.float32) + jnp.dot(
            attn, held[at], preferred_element_type=jnp.float32
        )
        mixed_ref[:, span] = mixed
        squares = squares + jnp.sum(mixed * mixed, axis=1, keepdims=True)
    scale = lax.rsqrt(squares / width + EPSILON)
    normed_ref[...] = (mixed_ref[...] * scale * gain_ref[...]).astype(jnp.bfloat16)


def mixture_kernel(
    offset,
    index_ref,
    first_ref,
    second_ref,
    back_ref,
    router_ref,
    up_a,
    up_b,
    in_a,
    in_b,
    down_a,
    down_b,
    out_a,
    out_b,
    first_out,
    second_out,
):
    rows, width = first_ref.shape
    own = (index_ref[0] & 1).astype(jnp.float32)

    def expert(mask):
        ids = back_ref[(index_ref[0] ^ mask) >> 1, rows : rows + 16, :].astype(jnp.float32)[0:1, :]
        return jnp.transpose(jnp.broadcast_to(ids, (rows, rows)))[:, 0:1]

    normed = jnp.concatenate([first_ref[...], second_ref[...]], axis=0)
    chosen = jnp.concatenate([expert(offset), expert(offset | 2)], axis=0)
    mine = chosen == own
    router = router_ref[...].astype(jnp.float32)
    column = jnp.where(chosen > 0, router[1:2, :], router[0:1, :])
    logits = jnp.sum(normed.astype(jnp.float32) * column, axis=1, keepdims=True)
    gate = jax.nn.sigmoid(logits)

    def hidden(weights):
        return jax.nn.gelu(jnp.dot(normed, weights[...], preferred_element_type=jnp.float32))

    mlp_a = hidden(up_a).astype(jnp.bfloat16)
    mlp_b = hidden(up_b).astype(jnp.bfloat16)
    exp_a = jnp.where(mine, hidden(in_a), 0.0).astype(jnp.bfloat16)
    exp_b = jnp.where(mine, 0.0, hidden(in_b)).astype(jnp.bfloat16)
    contract = (((1,), (1,)), ((), ()))
    step = min(width, 512)
    for begin in range(0, width, step):
        span = slice(begin, begin + step)
        part = gate * (
            jnp.dot(exp_a, out_a[:, span], preferred_element_type=jnp.float32)
            + jnp.dot(exp_b, out_b[:, span], preferred_element_type=jnp.float32)
        )
        part = part + (
            lax.dot_general(mlp_a, down_a[span, :], contract, preferred_element_type=jnp.float32)
            + lax.dot_general(mlp_b, down_b[span, :], contract, preferred_element_type=jnp.float32)
        )
        part = part.astype(jnp.bfloat16)
        first_out[:, span] = part[:rows]
        second_out[:, span] = part[rows:]


def body_by_pairs(
    queries,
    keys,
    values,
    resid,
    out_proj,
    norm_gain,
    up_proj,
    down_proj,
    router,
    expert_ids,
    expert_in,
    expert_out,
):
    rows, width = resid.shape
    heads = queries.shape[1] // DH
    ctx_count = lax.axis_size("ctx")
    device_index = lax.axis_index("ctx")
    index = device_index.reshape(1)
    exchange = functools.partial(
        lax.all_to_all,
        axis_name="ctx",
        split_axis=0,
        concat_axis=0,
        tiled=True,
        axis_index_groups=[list(range(parity, ctx_count, 2)) for parity in range(2)],
    )
    shape = jax.ShapeDtypeStruct
    packed = call(
        pack_kernel,
        [shape((rows, 3 * DH), jnp.bfloat16)] * heads,
        [SMEM] + [HBM] * 3,
        0,
        62,
        index,
        queries,
        keys,
        values,
        copies=3 * heads,
    )
    blocks = [packed[0]] + [swap(packed[at], 2 * at) for at in range(1, heads)]
    query, own = call(
        arrange_kernel,
        [shape((heads, rows, DH), jnp.bfloat16), shape((heads, rows, 2 * DH), jnp.bfloat16)],
        [SMEM] + [VMEM] * heads,
        0,
        8,
        index,
        *blocks,
    )
    other = swap(own, 1)
    weights_own = (up_proj, expert_in[0], down_proj, expert_out[0])
    weights_other = [swap(array, 1) for array in weights_own]
    weights_own = load(51, *weights_own)
    weights_other = load(44, *weights_other)
    weights = tuple(w for pair in zip(weights_own, weights_other) for w in pair)
    (out,) = call(
        attention_kernel,
        [shape((heads, rows + 16, DH), jnp.bfloat16)],
        [SMEM] + [VMEM] * 4,
        10**9,
        12,
        index,
        query,
        own,
        other,
        expert_ids.reshape(1, rows),
    )
    back = exchange(out)
    pieces = 4
    mixed, normed = call(
        project_kernel,
        [pltpu.VMEM((rows, width), jnp.float32), shape((rows, width), jnp.bfloat16)],
        [HBM, HBM, HBM, VMEM],
        2 * out_proj.size * rows,
        58,
        back,
        out_proj,
        resid,
        norm_gain.reshape(1, width),
        copies=pieces + 2,
        scratch=[
            pltpu.VMEM((pieces, out_proj.shape[0], width // pieces), out_proj.dtype),
            pltpu.VMEM(back.shape, back.dtype),
            pltpu.VMEM(resid.shape, resid.dtype),
        ],
    )
    units = sum(w.size for w in weights[:4]) // width

    def mix(offset, first, second):
        return call(
            functools.partial(mixture_kernel, offset),
            [pltpu.VMEM((rows, width), jnp.bfloat16)] * 2,
            [SMEM] + [VMEM] * 12,
            8 * rows * width * units,
            16,
            index,
            first,
            second,
            back,
            router.T,
            *weights,
        )

    def plus(first, second):
        return first.astype(jnp.float32) + second.astype(jnp.float32)

    far = [4 * at for at in range(ctx_count // 4 - 1, 1, -1)]
    gathered = {offset: swap(normed, offset) for offset in far}
    across = swap(normed, 2)
    beside = swap(normed, 4)
    beside_across = swap(across, 4)
    total = mixed
    for offset in far:
        first = gathered[offset]
        part, part_across = mix(offset, first, swap(first, 2))
        summed = plus(part, swap(part_across, 2)).astype(jnp.bfloat16)
        total = total + swap(summed, offset).astype(jnp.float32)
    part, part_across = mix(0, normed, across)
    part_beside, part_both = mix(4, beside, beside_across)
    summed = plus(part_across, swap(part_both, 4)).astype(jnp.bfloat16)
    total = total + plus(part, swap(part_beside, 4))
    total = total + swap(summed, 2).astype(jnp.float32)
    return total.astype(jnp.bfloat16)


def solution(mesh):
    ctx_count = mesh.shape["ctx"]

    def by_pairs(args):
        queries, router = args[0], args[8]
        return (
            router.shape[1] == 2
            and ctx_count == 2 * SPLIT
            and queries.shape[1] == ctx_count // 2 * DH
            and ctx_count % 4 == 0
            and ctx_count & (ctx_count - 1) == 0
        )

    def chosen(*args):
        if not by_pairs(args):
            return body(*args)
        return body_by_pairs(*args)

    placed = (
        P(("groups", "ctx"), None),
        P(("groups", "ctx"), None),
        P(("groups", "ctx"), None),
        P(("groups", "ctx"), None),
        P(),
        P(),
        P(None, "ctx"),
        P(None, "ctx"),
        P(),
        P(("groups", "ctx"), None),
        P("ctx", None, None),
        P("ctx", None, None),
    )
    return jax.shard_map(
        chosen, mesh=mesh, in_specs=placed, out_specs=P(("groups", "ctx"), None), check_vma=False
    )
```

```python
import functools
import jax
import jax.numpy as jnp
from jax import lax
from jax.experimental import pallas as pl
from jax.experimental.pallas import tpu as pltpu
from jax.sharding import PartitionSpec as P

DH = 128
SPLIT = 8


NEG_FILL = -1e30
EPSILON = 1e-06


def from_partner(array, axis, apart):
    return lax.ppermute(array, axis, [(i, i ^ 1 << apart) for i in range(lax.axis_size(axis))])


def update_state(state, query_rows, query_offset, key_block, value_block, key_offset):
    maxima, totals, numer = state
    count_query = query_rows.shape[0]
    count_keys = key_block.shape[0]
    head_count = query_rows.shape[1] // DH
    query_heads = query_rows.reshape(count_query, head_count, DH)
    key_heads = key_block.reshape(count_keys, head_count, DH)
    value_heads = value_block.reshape(count_keys, head_count, DH)
    scores = jnp.einsum(
        "qhd,khd->hqk", query_heads, key_heads, preferred_element_type=jnp.float32
    ) * DH ** (-0.5)
    query_positions = query_offset + jnp.arange(count_query, dtype=jnp.int32)
    key_positions = key_offset + jnp.arange(count_keys, dtype=jnp.int32)
    visible = (key_positions[None, :] <= query_positions[:, None])[None]
    masked = jnp.where(visible, scores, NEG_FILL)
    new_max = jnp.maximum(maxima, jnp.max(masked, axis=2))
    weights = jnp.where(visible, jnp.exp(masked - new_max[..., None]), 0.0)
    factor = jnp.exp(maxima - new_max)
    totals = totals * factor + jnp.sum(weights, axis=2)
    numer = numer * factor[..., None] + jnp.einsum(
        "hqk,khd->hqd",
        weights.astype(jnp.bfloat16),
        value_heads,
        preferred_element_type=jnp.float32,
    )
    return (new_max, totals, numer)


def attend(query_sets, keys, values):
    head_count = keys.shape[1] // DH
    initial = []
    for query_rows, query_offset in query_sets:
        count_query = query_rows.shape[0]
        initial.append(
            (
                jnp.full((head_count, count_query), NEG_FILL, jnp.float32),
                jnp.zeros((head_count, count_query), jnp.float32),
                jnp.zeros((head_count, count_query, DH), jnp.float32),
            )
        )
    states = tuple(initial)
    key_offset = jnp.int32(0)
    key_whole = lax.all_gather(keys, "ctx", axis=0, tiled=True)
    value_whole = lax.all_gather(values, "ctx", axis=0, tiled=True)
    total_keys = key_whole.shape[0]
    step_rows = min(total_keys, 1024)
    for begin in range(0, total_keys, step_rows):
        key_block = key_whole[begin : begin + step_rows]
        value_block = value_whole[begin : begin + step_rows]
        block_offset = key_offset + begin
        query_rows, query_offset = query_sets[0]
        needed = block_offset <= query_offset + query_rows.shape[0] - 1
        updated = [
            lax.cond(
                needed,
                lambda carried, rows_now=query_rows, offset_now=query_offset, keys_now=key_block, values_now=value_block, start_now=block_offset: update_state(
                    carried, rows_now, offset_now, keys_now, values_now, start_now
                ),
                lambda carried: carried,
                states[0],
            )
        ]
        states = tuple(updated)
    results = []
    for maxima, totals, numer in states:
        result = (numer / totals[..., None]).astype(jnp.bfloat16)
        results.append(
            jnp.transpose(result, (1, 0, 2)).reshape(result.shape[1], result.shape[0] * DH)
        )
    return results


def body(
    queries,
    keys,
    values,
    resid,
    out_proj,
    norm_gain,
    up_proj,
    down_proj,
    router,
    expert_ids,
    expert_in,
    expert_out,
):
    tok_rows = queries.shape[0]
    width = resid.shape[1]
    live_count = router.shape[1]
    ctx_count = lax.axis_size("ctx")
    device_index = lax.axis_index("ctx")
    base_offset = device_index * tok_rows
    attn = attend([(queries, base_offset)], keys, values)[0]
    mixed = resid.astype(jnp.float32) + jnp.dot(attn, out_proj, preferred_element_type=jnp.float32)
    normed = (
        mixed * lax.rsqrt(jnp.mean(mixed * mixed, axis=1, keepdims=True) + EPSILON) * norm_gain
    ).astype(jnp.bfloat16)
    mlp_blocks = jnp.stack([up_proj, down_proj], 0)
    for level in range(live_count.bit_length() - 1):
        other_block = from_partner(mlp_blocks, "ctx", level)
        mlp_blocks = jnp.concatenate([mlp_blocks, other_block], axis=2)
    slots_per = max(2, 5 * tok_rows // (4 * live_count))
    chosen = expert_ids[:, 0]
    onehot = (chosen[:, None] == jnp.arange(live_count, dtype=jnp.int32)[None, :]).astype(
        jnp.bfloat16
    )
    row_iota = jnp.arange(tok_rows, dtype=jnp.int32)
    strictly_lower = (row_iota[None, :] < row_iota[:, None]).astype(jnp.bfloat16)
    counts_before = jnp.dot(strictly_lower, onehot, preferred_element_type=jnp.float32)
    slot_index = jnp.sum(onehot.astype(jnp.float32) * counts_before, axis=1).astype(jnp.int32)
    target_slot = chosen * slots_per + slot_index
    dispatch_matrix = (
        jnp.arange(live_count * slots_per, dtype=jnp.int32)[:, None] == target_slot[None, :]
    ).astype(jnp.bfloat16)
    packed = jnp.dot(dispatch_matrix, normed, preferred_element_type=jnp.float32).astype(
        jnp.bfloat16
    )
    sending = jnp.broadcast_to(
        packed.reshape(1, live_count, slots_per, width), (SPLIT, live_count, slots_per, width)
    )
    sending = sending.reshape(ctx_count, 1, slots_per, width)
    own_expert = device_index % live_count
    router_column = lax.dynamic_slice_in_dim(router, own_expert, 1, 1)
    weight_in = expert_in[0]
    weight_out = expert_out[0]
    received = lax.all_to_all(sending, "ctx", split_axis=0, concat_axis=1, tiled=True)
    rows = received.reshape(-1, width)
    expert_hidden = jax.nn.gelu(
        jnp.dot(rows, weight_in, preferred_element_type=jnp.float32)
    ).astype(jnp.bfloat16)
    mlp_hidden = jax.nn.gelu(
        jnp.dot(rows, mlp_blocks[0], preferred_element_type=jnp.float32)
    ).astype(jnp.bfloat16)
    gate = jax.nn.sigmoid(jnp.dot(rows, router_column, preferred_element_type=jnp.float32))
    produced = gate * jnp.dot(expert_hidden, weight_out, preferred_element_type=jnp.float32)
    produced = produced + lax.dot_general(
        mlp_hidden, mlp_blocks[1], (((1,), (1,)), ((), ())), preferred_element_type=jnp.float32
    )
    came_back = lax.all_to_all(
        produced.astype(jnp.bfloat16).reshape(received.shape),
        "ctx",
        split_axis=1,
        concat_axis=0,
        tiled=True,
    )
    summed = jnp.sum(
        came_back.astype(jnp.float32).reshape(SPLIT, live_count * slots_per, width), axis=0
    )
    mixture_part = lax.dot_general(
        dispatch_matrix.astype(jnp.float32),
        summed,
        (((0,), (0,)), ((), ())),
        precision=lax.Precision.HIGHEST,
        preferred_element_type=jnp.float32,
    )
    return (mixed + mixture_part).astype(jnp.bfloat16)


def swap(array, mask):
    return lax.ppermute(array, "ctx", [(i, i ^ mask) for i in range(lax.axis_size("ctx"))])


VMEM = pl.BlockSpec(memory_space=pltpu.VMEM)
SMEM = pl.BlockSpec(memory_space=pltpu.SMEM)


HBM = pl.BlockSpec(memory_space=pltpu.HBM)


def call(kernel, outs, specs, flops, mib, *operands, copies=0, scratch=()):
    return pl.pallas_call(
        kernel,
        out_shape=outs,
        in_specs=specs,
        out_specs=[VMEM] * len(outs),
        scratch_shapes=[*scratch] + ([pltpu.SemaphoreType.DMA((copies,))] if copies else []),
        compiler_params=pltpu.CompilerParams(vmem_limit_bytes=mib * 2**20),
        cost_estimate=pl.CostEstimate(
            flops=flops,
            bytes_accessed=sum(x.size * x.dtype.itemsize for x in operands),
            transcendentals=0,
        ),
    )(*operands)


def copy_all(pairs, sems):
    copies = [pltpu.make_async_copy(a, b, sems.at[at]) for at, (a, b) in enumerate(pairs)]
    for copy in copies:
        copy.start()
    for copy in copies:
        copy.wait()


def load_kernel(*refs):
    count = len(refs) // 2
    copy_all(zip(refs[:count], refs[count : 2 * count]), refs[-1])


def load(mib, *arrays):
    outs = [pltpu.VMEM(array.shape, array.dtype) for array in arrays]
    count = len(arrays)
    return call(load_kernel, outs, [HBM] * count, 0, mib, *arrays, copies=count)


def pack_kernel(index_ref, query_ref, key_ref, value_ref, *refs):
    pairs = []
    for at, out_ref in enumerate(refs[:-1]):
        head = (index_ref[0] ^ 2 * at) >> 1
        columns = pl.ds(pl.multiple_of(head * DH, DH), DH)
        for part, ref in enumerate((query_ref, key_ref, value_ref)):
            pairs.append((ref.at[:, columns], out_ref.at[:, pl.ds(part * DH, DH)]))
    copy_all(pairs, refs[-1])


def arrange_kernel(index_ref, *refs):
    query_ref, pair_ref = refs[-2:]
    for at, ref in enumerate(refs[:-2]):
        place = (index_ref[0] ^ 2 * at) >> 1
        query_ref[place] = ref[:, :DH]
        pair_ref[place] = ref[:, DH:]


def attention_kernel(index_ref, query_ref, own_ref, other_ref, ids_ref, *refs):
    out_refs, (held, ids, sem) = refs[:-3], refs[-3:]
    ids_copy = pltpu.make_async_copy(ids_ref, ids, sem.at[0])
    ids_copy.start()
    blocks, rows, _ = own_ref.shape
    row_at = lax.broadcasted_iota(jnp.int32, (rows, rows), 0)
    column_at = lax.broadcasted_iota(jnp.int32, (rows, rows), 1)
    causal = column_at <= row_at
    also = jnp.broadcast_to(index_ref[0] & 1 == 1, (rows, rows))
    contract = (((1,), (1,)), ((), ()))
    for block in range(blocks):
        query = query_ref[block]
        scores = []
        for ref, last_visible in ((own_ref, causal), (other_ref, also)):
            for at in range(block + 1):
                score = lax.dot_general(
                    query, ref[at, :, :DH], contract, preferred_element_type=jnp.float32
                ) * DH ** (-0.5)
                if at == block:
                    score = jnp.where(last_visible, score, NEG_FILL)
                scores.append(score)
        peak = scores[0]
        for score in scores[1:]:
            peak = jnp.maximum(peak, score)
        row_max = jnp.max(peak, axis=1, keepdims=True)
        numer = jnp.zeros((rows, DH), jnp.float32)
        summed = jnp.zeros((rows, rows), jnp.float32)
        for at, score in enumerate(scores):
            weights = jnp.exp(score - row_max)
            summed = summed + weights
            ref = own_ref if at <= block else other_ref
            numer = numer + jnp.dot(
                weights.astype(jnp.bfloat16),
                ref[at % (block + 1), :, DH:],
                preferred_element_type=jnp.float32,
            )
        totals = jnp.sum(summed, axis=1, keepdims=True)
        held[block] = (numer / totals).astype(jnp.bfloat16)
    ids_copy.wait()
    id_rows = jnp.broadcast_to(
        ids[...].astype(jnp.float32), (out_refs[0].shape[0] - rows, rows)
    ).astype(jnp.bfloat16)
    for at, out_ref in enumerate(out_refs):
        out_ref[:rows, :] = held[(index_ref[0] ^ 2 * at) >> 1]
        out_ref[rows:, :] = id_rows


def project_kernel(index_ref, weight_ref, resid_ref, gain_ref, *refs):
    heads_in, (mixed_ref, normed_ref, top_ref, bottom_ref, held) = refs[:-5], refs[-5:]
    rows = resid_ref.shape[0]
    for at, ref in enumerate(heads_in):
        held[(index_ref[0] ^ 2 * at) >> 1] = ref[:rows, :]
    attn = jnp.concatenate([held[head] for head in range(len(heads_in))], axis=1)
    mixed = resid_ref[...].astype(jnp.float32) + jnp.dot(
        attn, weight_ref[...], preferred_element_type=jnp.float32
    )
    mixed_ref[...] = mixed
    scale = lax.rsqrt(jnp.mean(mixed * mixed, axis=1, keepdims=True) + EPSILON)
    normed = (mixed * scale * gain_ref[...]).astype(jnp.bfloat16)
    normed_ref[...] = normed
    top_ref[...] = normed[: rows // 2]
    bottom_ref[...] = normed[rows // 2 :]


def mixture_kernel(
    start, index_ref, router_ref, up_a, up_b, in_a, in_b, down_a, down_b, out_a, out_b, *refs
):
    count = len(refs) // 3
    shards, ids_refs, out_refs = refs[:count], refs[count : 2 * count], refs[2 * count :]
    rows, width = shards[0].shape
    own = (index_ref[0] & 1).astype(jnp.float32)

    def expert(ref):
        count = ref.shape[1]
        ids = ref[count : count + 16, :].astype(jnp.float32)[0:1, :]
        column = jnp.transpose(jnp.broadcast_to(ids, (count, count)))[:, 0:1]
        return column[start : start + rows]

    normed = jnp.concatenate([ref[...] for ref in shards], axis=0)
    chosen = jnp.concatenate([expert(ref) for ref in ids_refs], axis=0)
    mine = chosen == own
    router = router_ref[...].astype(jnp.float32)
    column = jnp.where(chosen > 0, router[1:2, :], router[0:1, :])
    logits = jnp.sum(normed.astype(jnp.float32) * column, axis=1, keepdims=True)
    gate = jax.nn.sigmoid(logits)

    def hidden(weights):
        return jax.nn.gelu(jnp.dot(normed, weights[...], preferred_element_type=jnp.float32))

    mlp_a = hidden(up_a).astype(jnp.bfloat16)
    mlp_b = hidden(up_b).astype(jnp.bfloat16)
    exp_a = jnp.where(mine, hidden(in_a), 0.0).astype(jnp.bfloat16)
    exp_b = jnp.where(mine, 0.0, hidden(in_b)).astype(jnp.bfloat16)
    contract = (((1,), (1,)), ((), ()))
    step = min(width, 512)
    for begin in range(0, width, step):
        span = slice(begin, begin + step)
        part = gate * (
            jnp.dot(exp_a, out_a[:, span], preferred_element_type=jnp.float32)
            + jnp.dot(exp_b, out_b[:, span], preferred_element_type=jnp.float32)
        )
        part = part + (
            lax.dot_general(mlp_a, down_a[span, :], contract, preferred_element_type=jnp.float32)
            + lax.dot_general(mlp_b, down_b[span, :], contract, preferred_element_type=jnp.float32)
        )
        part = part.astype(jnp.bfloat16)
        for at, out_ref in enumerate(out_refs):
            out_ref[:, span] = part[at * rows : (at + 1) * rows]


def finish_kernel(mixed_ref, *refs):
    whole, split, out_ref = refs[:3], refs[3:-1], refs[-1]
    rows = mixed_ref.shape[0]
    for at in range(2):
        span = slice(at * rows // 2, (at + 1) * rows // 2)
        total = mixed_ref[span, :]
        for ref in whole:
            total = total + ref[span, :].astype(jnp.float32)
        for ref in split[at::2]:
            total = total + ref[...].astype(jnp.float32)
        out_ref[span, :] = total.astype(jnp.bfloat16)


def body_by_pairs(
    queries,
    keys,
    values,
    resid,
    out_proj,
    norm_gain,
    up_proj,
    down_proj,
    router,
    expert_ids,
    expert_in,
    expert_out,
):
    rows, width = resid.shape
    heads = queries.shape[1] // DH
    ctx_count = lax.axis_size("ctx")
    device_index = lax.axis_index("ctx")
    index = device_index.reshape(1)
    shape = jax.ShapeDtypeStruct
    packed = call(
        pack_kernel,
        [pltpu.VMEM((rows, 3 * DH), jnp.bfloat16)] * heads,
        [SMEM] + [HBM] * 3,
        0,
        62,
        index,
        queries,
        keys,
        values,
        copies=3 * heads,
    )
    blocks = [packed[0]] + [swap(packed[at], 2 * at) for at in range(1, heads)]
    query, own = call(
        arrange_kernel,
        [shape((heads, rows, DH), jnp.bfloat16), shape((heads, rows, 2 * DH), jnp.bfloat16)],
        [SMEM] + [VMEM] * heads,
        0,
        8,
        index,
        *blocks,
    )
    other = swap(own, 1)
    weights_own = (up_proj, expert_in[0], down_proj, expert_out[0])
    weights_other = [swap(array, 1) for array in weights_own]
    *weights_own, out_weight, resid_rows = load(44, *weights_own, out_proj, resid)
    weights = tuple(w for pair in zip(weights_own, weights_other) for w in pair)
    outs = call(
        attention_kernel,
        [pltpu.VMEM((rows + 16, DH), jnp.bfloat16)] * heads,
        [SMEM] + [VMEM] * 3 + [HBM],
        10**9,
        12,
        index,
        query,
        own,
        other,
        expert_ids.reshape(1, rows),
        copies=1,
        scratch=[pltpu.VMEM((heads, rows, DH), jnp.bfloat16), pltpu.VMEM((1, rows), jnp.int32)],
    )
    backs = [outs[0]] + [swap(outs[at], 2 * at) for at in range(1, heads)]
    mixed, normed, *halves = call(
        project_kernel,
        [pltpu.VMEM((rows, width), jnp.float32), pltpu.VMEM((rows, width), jnp.bfloat16)]
        + [pltpu.VMEM((rows // 2, width), jnp.bfloat16)] * 2,
        [SMEM] + [VMEM] * (heads + 3),
        2 * out_proj.size * rows,
        12,
        index,
        out_weight,
        resid_rows,
        norm_gain.reshape(1, width),
        *backs,
        scratch=[pltpu.VMEM((heads, rows, DH), jnp.bfloat16)],
    )
    units = sum(w.size for w in weights[:4]) // width

    def mix(shards, start=0):
        count = next(iter(shards.values())).shape[0]
        return call(
            functools.partial(mixture_kernel, start),
            [pltpu.VMEM((count, width), jnp.bfloat16)] * len(shards),
            [SMEM] + [VMEM] * (9 + 2 * len(shards)),
            4 * len(shards) * count * width * units,
            16,
            index,
            router.T,
            *weights,
            *shards.values(),
            *(backs[offset // 2] for offset in shards),
        )

    def plus(first, second):
        return (first.astype(jnp.float32) + second.astype(jnp.float32)).astype(jnp.bfloat16)

    far = [4 * at for at in range(ctx_count // 4 - 1, 1, -1)]
    across = swap(normed, 2)
    beside = swap(normed, 4)
    beside_across = swap(across, 4)
    arrived = []
    for offset in far:
        for half, rows_sent in zip("ab", halves):
            first = swap(rows_sent, offset)
            second = swap(first, 2)
            start = 0 if half == "a" else rows // 2
            part, part_across = mix({offset: first, offset | 2: second}, start)
            summed = plus(part, swap(part_across, 2))
            arrived.append(swap(summed, offset))
    part, part_across = mix({0: normed, 2: across})
    part_beside, part_both = mix({4: beside, 6: beside_across})
    summed = plus(part_across, swap(part_both, 4))
    (result,) = call(
        finish_kernel,
        [shape((rows, width), jnp.bfloat16)],
        [VMEM] * (4 + len(arrived)),
        0,
        12,
        mixed,
        part,
        swap(part_beside, 4),
        swap(summed, 2),
        *arrived,
    )
    return result


def solution(mesh):
    ctx_count = mesh.shape["ctx"]

    def by_pairs(args):
        queries, router = args[0], args[8]
        return (
            router.shape[1] == 2
            and ctx_count == 2 * SPLIT
            and queries.shape[1] == ctx_count // 2 * DH
            and ctx_count % 4 == 0
            and ctx_count & (ctx_count - 1) == 0
        )

    def chosen(*args):
        if not by_pairs(args):
            return body(*args)
        return body_by_pairs(*args)

    placed = (
        P(("groups", "ctx"), None),
        P(("groups", "ctx"), None),
        P(("groups", "ctx"), None),
        P(("groups", "ctx"), None),
        P(),
        P(),
        P(None, "ctx"),
        P(None, "ctx"),
        P(),
        P(("groups", "ctx"), None),
        P("ctx", None, None),
        P("ctx", None, None),
    )
    return jax.shard_map(
        chosen, mesh=mesh, in_specs=placed, out_specs=P(("groups", "ctx"), None), check_vma=False
    )
```

```python
import functools
import jax
import jax.numpy as jnp
from jax import lax
from jax.experimental import pallas as pl
from jax.experimental.pallas import tpu as pltpu
from jax.sharding import PartitionSpec as P

DH = 128
SPLIT = 8


NEG_FILL = -1e30
EPSILON = 1e-06


def from_partner(array, axis, apart):
    return lax.ppermute(array, axis, [(i, i ^ 1 << apart) for i in range(lax.axis_size(axis))])


def update_state(state, query_rows, query_offset, key_block, value_block, key_offset):
    maxima, totals, numer = state
    count_query = query_rows.shape[0]
    count_keys = key_block.shape[0]
    head_count = query_rows.shape[1] // DH
    query_heads = query_rows.reshape(count_query, head_count, DH)
    key_heads = key_block.reshape(count_keys, head_count, DH)
    value_heads = value_block.reshape(count_keys, head_count, DH)
    scores = jnp.einsum(
        "qhd,khd->hqk", query_heads, key_heads, preferred_element_type=jnp.float32
    ) * DH ** (-0.5)
    query_positions = query_offset + jnp.arange(count_query, dtype=jnp.int32)
    key_positions = key_offset + jnp.arange(count_keys, dtype=jnp.int32)
    visible = (key_positions[None, :] <= query_positions[:, None])[None]
    masked = jnp.where(visible, scores, NEG_FILL)
    new_max = jnp.maximum(maxima, jnp.max(masked, axis=2))
    weights = jnp.where(visible, jnp.exp(masked - new_max[..., None]), 0.0)
    factor = jnp.exp(maxima - new_max)
    totals = totals * factor + jnp.sum(weights, axis=2)
    numer = numer * factor[..., None] + jnp.einsum(
        "hqk,khd->hqd",
        weights.astype(jnp.bfloat16),
        value_heads,
        preferred_element_type=jnp.float32,
    )
    return (new_max, totals, numer)


def attend(query_sets, keys, values):
    head_count = keys.shape[1] // DH
    initial = []
    for query_rows, query_offset in query_sets:
        count_query = query_rows.shape[0]
        initial.append(
            (
                jnp.full((head_count, count_query), NEG_FILL, jnp.float32),
                jnp.zeros((head_count, count_query), jnp.float32),
                jnp.zeros((head_count, count_query, DH), jnp.float32),
            )
        )
    states = tuple(initial)
    key_offset = jnp.int32(0)
    key_whole = lax.all_gather(keys, "ctx", axis=0, tiled=True)
    value_whole = lax.all_gather(values, "ctx", axis=0, tiled=True)
    total_keys = key_whole.shape[0]
    step_rows = min(total_keys, 1024)
    for begin in range(0, total_keys, step_rows):
        key_block = key_whole[begin : begin + step_rows]
        value_block = value_whole[begin : begin + step_rows]
        block_offset = key_offset + begin
        query_rows, query_offset = query_sets[0]
        needed = block_offset <= query_offset + query_rows.shape[0] - 1
        updated = [
            lax.cond(
                needed,
                lambda carried, rows_now=query_rows, offset_now=query_offset, keys_now=key_block, values_now=value_block, start_now=block_offset: update_state(
                    carried, rows_now, offset_now, keys_now, values_now, start_now
                ),
                lambda carried: carried,
                states[0],
            )
        ]
        states = tuple(updated)
    results = []
    for maxima, totals, numer in states:
        result = (numer / totals[..., None]).astype(jnp.bfloat16)
        results.append(
            jnp.transpose(result, (1, 0, 2)).reshape(result.shape[1], result.shape[0] * DH)
        )
    return results


def body(
    queries,
    keys,
    values,
    resid,
    out_proj,
    norm_gain,
    up_proj,
    down_proj,
    router,
    expert_ids,
    expert_in,
    expert_out,
):
    tok_rows = queries.shape[0]
    width = resid.shape[1]
    live_count = router.shape[1]
    ctx_count = lax.axis_size("ctx")
    device_index = lax.axis_index("ctx")
    base_offset = device_index * tok_rows
    attn = attend([(queries, base_offset)], keys, values)[0]
    mixed = resid.astype(jnp.float32) + jnp.dot(attn, out_proj, preferred_element_type=jnp.float32)
    normed = (
        mixed * lax.rsqrt(jnp.mean(mixed * mixed, axis=1, keepdims=True) + EPSILON) * norm_gain
    ).astype(jnp.bfloat16)
    mlp_blocks = jnp.stack([up_proj, down_proj], 0)
    for level in range(live_count.bit_length() - 1):
        other_block = from_partner(mlp_blocks, "ctx", level)
        mlp_blocks = jnp.concatenate([mlp_blocks, other_block], axis=2)
    slots_per = max(2, 5 * tok_rows // (4 * live_count))
    chosen = expert_ids[:, 0]
    onehot = (chosen[:, None] == jnp.arange(live_count, dtype=jnp.int32)[None, :]).astype(
        jnp.bfloat16
    )
    row_iota = jnp.arange(tok_rows, dtype=jnp.int32)
    strictly_lower = (row_iota[None, :] < row_iota[:, None]).astype(jnp.bfloat16)
    counts_before = jnp.dot(strictly_lower, onehot, preferred_element_type=jnp.float32)
    slot_index = jnp.sum(onehot.astype(jnp.float32) * counts_before, axis=1).astype(jnp.int32)
    target_slot = chosen * slots_per + slot_index
    dispatch_matrix = (
        jnp.arange(live_count * slots_per, dtype=jnp.int32)[:, None] == target_slot[None, :]
    ).astype(jnp.bfloat16)
    packed = jnp.dot(dispatch_matrix, normed, preferred_element_type=jnp.float32).astype(
        jnp.bfloat16
    )
    sending = jnp.broadcast_to(
        packed.reshape(1, live_count, slots_per, width), (SPLIT, live_count, slots_per, width)
    )
    sending = sending.reshape(ctx_count, 1, slots_per, width)
    own_expert = device_index % live_count
    router_column = lax.dynamic_slice_in_dim(router, own_expert, 1, 1)
    weight_in = expert_in[0]
    weight_out = expert_out[0]
    received = lax.all_to_all(sending, "ctx", split_axis=0, concat_axis=1, tiled=True)
    rows = received.reshape(-1, width)
    expert_hidden = jax.nn.gelu(
        jnp.dot(rows, weight_in, preferred_element_type=jnp.float32)
    ).astype(jnp.bfloat16)
    mlp_hidden = jax.nn.gelu(
        jnp.dot(rows, mlp_blocks[0], preferred_element_type=jnp.float32)
    ).astype(jnp.bfloat16)
    gate = jax.nn.sigmoid(jnp.dot(rows, router_column, preferred_element_type=jnp.float32))
    produced = gate * jnp.dot(expert_hidden, weight_out, preferred_element_type=jnp.float32)
    produced = produced + lax.dot_general(
        mlp_hidden, mlp_blocks[1], (((1,), (1,)), ((), ())), preferred_element_type=jnp.float32
    )
    came_back = lax.all_to_all(
        produced.astype(jnp.bfloat16).reshape(received.shape),
        "ctx",
        split_axis=1,
        concat_axis=0,
        tiled=True,
    )
    summed = jnp.sum(
        came_back.astype(jnp.float32).reshape(SPLIT, live_count * slots_per, width), axis=0
    )
    mixture_part = lax.dot_general(
        dispatch_matrix.astype(jnp.float32),
        summed,
        (((0,), (0,)), ((), ())),
        precision=lax.Precision.HIGHEST,
        preferred_element_type=jnp.float32,
    )
    return (mixed + mixture_part).astype(jnp.bfloat16)


LOG2_E = 1.4426950408889634


def swap(array, mask):
    return lax.ppermute(array, "ctx", [(i, i ^ mask) for i in range(lax.axis_size("ctx"))])


VMEM = pl.BlockSpec(memory_space=pltpu.VMEM)
SMEM = pl.BlockSpec(memory_space=pltpu.SMEM)


HBM = pl.BlockSpec(memory_space=pltpu.HBM)


def call(kernel, outs, specs, flops, mib, *operands, copies=0, scratch=()):
    return pl.pallas_call(
        kernel,
        out_shape=outs,
        in_specs=specs,
        out_specs=[VMEM] * len(outs),
        scratch_shapes=[*scratch] + ([pltpu.SemaphoreType.DMA((copies,))] if copies else []),
        compiler_params=pltpu.CompilerParams(vmem_limit_bytes=mib * 2**20),
        cost_estimate=pl.CostEstimate(
            flops=flops,
            bytes_accessed=sum(x.size * x.dtype.itemsize for x in operands),
            transcendentals=0,
        ),
    )(*operands)


def copy_all(pairs, sems):
    copies = [pltpu.make_async_copy(a, b, sems.at[at]) for at, (a, b) in enumerate(pairs)]
    for copy in copies:
        copy.start()
    for copy in copies:
        copy.wait()


def load_kernel(*refs):
    count = len(refs) // 2
    copy_all(zip(refs[:count], refs[count : 2 * count]), refs[-1])


def load(mib, *arrays):
    outs = [pltpu.VMEM(array.shape, array.dtype) for array in arrays]
    count = len(arrays)
    return call(load_kernel, outs, [HBM] * count, 0, mib, *arrays, copies=count)


def pack_kernel(index_ref, query_ref, key_ref, value_ref, *refs):
    pairs = []
    for at, out_ref in enumerate(refs[:-1]):
        head = (index_ref[0] ^ 2 * at) >> 1
        columns = pl.ds(pl.multiple_of(head * DH, DH), DH)
        for part, ref in enumerate((query_ref, key_ref, value_ref)):
            pairs.append((ref.at[:, columns], out_ref.at[:, pl.ds(part * DH, DH)]))
    copy_all(pairs, refs[-1])


def arrange_kernel(index_ref, *refs):
    query_ref, pair_ref = refs[-2:]
    for at, ref in enumerate(refs[:-2]):
        place = (index_ref[0] ^ 2 * at) >> 1
        query_ref[place] = ref[:, :DH]
        pair_ref[place] = ref[:, DH:]


def attention_kernel(index_ref, query_ref, own_ref, other_ref, ids_ref, *refs):
    out_refs, (held, ids, sem) = refs[:-3], refs[-3:]
    ids_copy = pltpu.make_async_copy(ids_ref, ids, sem.at[0])
    ids_copy.start()
    blocks, rows, _ = own_ref.shape
    row_at = lax.broadcasted_iota(jnp.int32, (rows, rows), 0)
    column_at = lax.broadcasted_iota(jnp.int32, (rows, rows), 1)
    causal = column_at <= row_at
    also = jnp.broadcast_to(index_ref[0] & 1 == 1, (rows, rows))
    contract = (((1,), (1,)), ((), ()))
    for block in range(blocks):
        query = query_ref[block]
        pair = []
        for ref, last_visible in ((own_ref, causal), (other_ref, also)):
            seen = ref[: block + 1].reshape((block + 1) * rows, 2 * DH)
            score = lax.dot_general(
                query, seen[:, :DH], contract, preferred_element_type=jnp.float32
            )
            last = jnp.where(last_visible, score[:, block * rows :], NEG_FILL)
            if block:
                score = jnp.concatenate([score[:, : block * rows], last], axis=1)
            else:
                score = last
            pair.append((score, seen[:, DH:]))
        row_max = jnp.maximum(
            *(jnp.max(score, axis=1, keepdims=True) for score, _ in pair)
        )
        numer, totals = 0.0, 0.0
        for score, value in pair:
            weights = jnp.exp2((score - row_max) * (DH ** (-0.5) * LOG2_E))
            totals = totals + jnp.sum(weights, axis=1, keepdims=True)
            numer = numer + jnp.dot(
                weights.astype(jnp.bfloat16), value, preferred_element_type=jnp.float32
            )
        held[block] = (numer / totals).astype(jnp.bfloat16)
    ids_copy.wait()
    id_rows = jnp.broadcast_to(
        ids[...].astype(jnp.float32), (out_refs[0].shape[0] - rows, rows)
    ).astype(jnp.bfloat16)
    for at, out_ref in enumerate(out_refs):
        out_ref[:rows, :] = held[(index_ref[0] ^ 2 * at) >> 1]
        out_ref[rows:, :] = id_rows


def project_kernel(index_ref, weight_ref, resid_ref, gain_ref, *refs):
    heads_in, (mixed_ref, normed_ref, top_ref, bottom_ref, held) = refs[:-5], refs[-5:]
    rows = resid_ref.shape[0]
    for at, ref in enumerate(heads_in):
        held[(index_ref[0] ^ 2 * at) >> 1] = ref[:rows, :]
    attn = jnp.concatenate([held[head] for head in range(len(heads_in))], axis=1)
    mixed = resid_ref[...].astype(jnp.float32) + jnp.dot(
        attn, weight_ref[...], preferred_element_type=jnp.float32
    )
    mixed_ref[...] = mixed
    scale = lax.rsqrt(jnp.mean(mixed * mixed, axis=1, keepdims=True) + EPSILON)
    normed = (mixed * scale * gain_ref[...]).astype(jnp.bfloat16)
    normed_ref[...] = normed
    top_ref[...] = normed[: rows // 2]
    bottom_ref[...] = normed[rows // 2 :]


def mixture_kernel(
    start, index_ref, router_ref, up_a, up_b, in_a, in_b, down_a, down_b, out_a, out_b, *refs
):
    count = len(refs) // 3
    shards, ids_refs, out_refs = refs[:count], refs[count : 2 * count], refs[2 * count :]
    rows, width = shards[0].shape
    own = (index_ref[0] & 1).astype(jnp.float32)

    def expert(ref):
        count = ref.shape[1]
        ids = ref[count : count + 16, :].astype(jnp.float32)[0:1, :]
        column = jnp.transpose(jnp.broadcast_to(ids, (count, count)))[:, 0:1]
        return column[start : start + rows]

    normed = jnp.concatenate([ref[...] for ref in shards], axis=0)
    chosen = jnp.concatenate([expert(ref) for ref in ids_refs], axis=0)
    mine = chosen == own
    router = router_ref[...].astype(jnp.float32)
    column = jnp.where(chosen > 0, router[1:2, :], router[0:1, :])
    logits = jnp.sum(normed.astype(jnp.float32) * column, axis=1, keepdims=True)
    gate = jax.nn.sigmoid(logits)

    def hidden(weights):
        return jax.nn.gelu(jnp.dot(normed, weights[...], preferred_element_type=jnp.float32))

    mlp_a = hidden(up_a).astype(jnp.bfloat16)
    mlp_b = hidden(up_b).astype(jnp.bfloat16)
    exp_a = jnp.where(mine, hidden(in_a), 0.0).astype(jnp.bfloat16)
    exp_b = jnp.where(mine, 0.0, hidden(in_b)).astype(jnp.bfloat16)
    contract = (((1,), (1,)), ((), ()))
    step = min(width, 512)
    for begin in range(0, width, step):
        span = slice(begin, begin + step)
        part = gate * (
            jnp.dot(exp_a, out_a[:, span], preferred_element_type=jnp.float32)
            + jnp.dot(exp_b, out_b[:, span], preferred_element_type=jnp.float32)
        )
        part = part + (
            lax.dot_general(mlp_a, down_a[span, :], contract, preferred_element_type=jnp.float32)
            + lax.dot_general(mlp_b, down_b[span, :], contract, preferred_element_type=jnp.float32)
        )
        part = part.astype(jnp.bfloat16)
        for at, out_ref in enumerate(out_refs):
            out_ref[:, span] = part[at * rows : (at + 1) * rows]


def finish_kernel(mixed_ref, *refs):
    whole, split, out_ref = refs[:3], refs[3:-1], refs[-1]
    rows = mixed_ref.shape[0]
    for at in range(2):
        span = slice(at * rows // 2, (at + 1) * rows // 2)
        total = mixed_ref[span, :]
        for ref in whole:
            total = total + ref[span, :].astype(jnp.float32)
        for ref in split[at::2]:
            total = total + ref[...].astype(jnp.float32)
        out_ref[span, :] = total.astype(jnp.bfloat16)


def body_by_pairs(
    queries,
    keys,
    values,
    resid,
    out_proj,
    norm_gain,
    up_proj,
    down_proj,
    router,
    expert_ids,
    expert_in,
    expert_out,
):
    rows, width = resid.shape
    heads = queries.shape[1] // DH
    ctx_count = lax.axis_size("ctx")
    device_index = lax.axis_index("ctx")
    index = device_index.reshape(1)
    shape = jax.ShapeDtypeStruct
    packed = call(
        pack_kernel,
        [pltpu.VMEM((rows, 3 * DH), jnp.bfloat16)] * heads,
        [SMEM] + [HBM] * 3,
        0,
        62,
        index,
        queries,
        keys,
        values,
        copies=3 * heads,
    )
    blocks = [packed[0]] + [swap(packed[at], 2 * at) for at in range(1, heads)]
    query, own = call(
        arrange_kernel,
        [shape((heads, rows, DH), jnp.bfloat16), shape((heads, rows, 2 * DH), jnp.bfloat16)],
        [SMEM] + [VMEM] * heads,
        0,
        8,
        index,
        *blocks,
    )
    other = swap(own, 1)
    weights_own = (up_proj, expert_in[0], down_proj, expert_out[0])
    weights_other = [swap(array, 1) for array in weights_own]
    *weights_own, out_weight, resid_rows = load(44, *weights_own, out_proj, resid)
    weights = tuple(w for pair in zip(weights_own, weights_other) for w in pair)
    outs = call(
        attention_kernel,
        [pltpu.VMEM((rows + 16, DH), jnp.bfloat16)] * heads,
        [SMEM] + [VMEM] * 3 + [HBM],
        10**9,
        12,
        index,
        query,
        own,
        other,
        expert_ids.reshape(1, rows),
        copies=1,
        scratch=[pltpu.VMEM((heads, rows, DH), jnp.bfloat16), pltpu.VMEM((1, rows), jnp.int32)],
    )
    backs = [outs[0]] + [swap(outs[at], 2 * at) for at in range(1, heads)]
    mixed, normed, *halves = call(
        project_kernel,
        [pltpu.VMEM((rows, width), jnp.float32), pltpu.VMEM((rows, width), jnp.bfloat16)]
        + [pltpu.VMEM((rows // 2, width), jnp.bfloat16)] * 2,
        [SMEM] + [VMEM] * (heads + 3),
        2 * out_proj.size * rows,
        12,
        index,
        out_weight,
        resid_rows,
        norm_gain.reshape(1, width),
        *backs,
        scratch=[pltpu.VMEM((heads, rows, DH), jnp.bfloat16)],
    )
    units = sum(w.size for w in weights[:4]) // width

    def mix(shards, start=0):
        count = next(iter(shards.values())).shape[0]
        return call(
            functools.partial(mixture_kernel, start),
            [pltpu.VMEM((count, width), jnp.bfloat16)] * len(shards),
            [SMEM] + [VMEM] * (9 + 2 * len(shards)),
            4 * len(shards) * count * width * units,
            16,
            index,
            router.T,
            *weights,
            *shards.values(),
            *(backs[offset // 2] for offset in shards),
        )

    def plus(first, second):
        return (first.astype(jnp.float32) + second.astype(jnp.float32)).astype(jnp.bfloat16)

    far = [4 * at for at in range(ctx_count // 4 - 1, 1, -1)]
    across = swap(normed, 2)
    beside = swap(normed, 4)
    beside_across = swap(across, 4)
    arrived = []
    for offset in far:
        for half, rows_sent in zip("ab", halves):
            first = swap(rows_sent, offset)
            second = swap(first, 2)
            start = 0 if half == "a" else rows // 2
            part, part_across = mix({offset: first, offset | 2: second}, start)
            summed = plus(part, swap(part_across, 2))
            arrived.append(swap(summed, offset))
    part, part_across = mix({0: normed, 2: across})
    (part_beside,) = mix({4: beside})
    (part_both,) = mix({6: beside_across})
    summed = plus(part_across, swap(part_both, 4))
    (result,) = call(
        finish_kernel,
        [shape((rows, width), jnp.bfloat16)],
        [VMEM] * (4 + len(arrived)),
        0,
        12,
        mixed,
        part,
        swap(part_beside, 4),
        swap(summed, 2),
        *arrived,
    )
    return result


def solution(mesh):
    ctx_count = mesh.shape["ctx"]

    def by_pairs(args):
        queries, router = args[0], args[8]
        return (
            router.shape[1] == 2
            and ctx_count == 2 * SPLIT
            and queries.shape[1] == ctx_count // 2 * DH
            and ctx_count % 4 == 0
            and ctx_count & (ctx_count - 1) == 0
        )

    def chosen(*args):
        if not by_pairs(args):
            return body(*args)
        return body_by_pairs(*args)

    placed = (
        P(("groups", "ctx"), None),
        P(("groups", "ctx"), None),
        P(("groups", "ctx"), None),
        P(("groups", "ctx"), None),
        P(),
        P(),
        P(None, "ctx"),
        P(None, "ctx"),
        P(),
        P(("groups", "ctx"), None),
        P("ctx", None, None),
        P("ctx", None, None),
    )
    return jax.shard_map(
        chosen, mesh=mesh, in_specs=placed, out_specs=P(("groups", "ctx"), None), check_vma=False
    )
```

```python
import functools
import jax
import jax.numpy as jnp
from jax import lax
from jax.experimental import pallas as pl
from jax.experimental.pallas import tpu as pltpu
from jax.sharding import PartitionSpec as P

DH = 128
SPLIT = 8


NEG_FILL = -1e30
EPSILON = 1e-06


def from_partner(array, axis, apart):
    return lax.ppermute(array, axis, [(i, i ^ 1 << apart) for i in range(lax.axis_size(axis))])


def update_state(state, query_rows, query_offset, key_block, value_block, key_offset):
    maxima, totals, numer = state
    count_query = query_rows.shape[0]
    count_keys = key_block.shape[0]
    head_count = query_rows.shape[1] // DH
    query_heads = query_rows.reshape(count_query, head_count, DH)
    key_heads = key_block.reshape(count_keys, head_count, DH)
    value_heads = value_block.reshape(count_keys, head_count, DH)
    scores = jnp.einsum(
        "qhd,khd->hqk", query_heads, key_heads, preferred_element_type=jnp.float32
    ) * DH ** (-0.5)
    query_positions = query_offset + jnp.arange(count_query, dtype=jnp.int32)
    key_positions = key_offset + jnp.arange(count_keys, dtype=jnp.int32)
    visible = (key_positions[None, :] <= query_positions[:, None])[None]
    masked = jnp.where(visible, scores, NEG_FILL)
    new_max = jnp.maximum(maxima, jnp.max(masked, axis=2))
    weights = jnp.where(visible, jnp.exp(masked - new_max[..., None]), 0.0)
    factor = jnp.exp(maxima - new_max)
    totals = totals * factor + jnp.sum(weights, axis=2)
    numer = numer * factor[..., None] + jnp.einsum(
        "hqk,khd->hqd",
        weights.astype(jnp.bfloat16),
        value_heads,
        preferred_element_type=jnp.float32,
    )
    return (new_max, totals, numer)


def attend(query_sets, keys, values):
    head_count = keys.shape[1] // DH
    initial = []
    for query_rows, query_offset in query_sets:
        count_query = query_rows.shape[0]
        initial.append(
            (
                jnp.full((head_count, count_query), NEG_FILL, jnp.float32),
                jnp.zeros((head_count, count_query), jnp.float32),
                jnp.zeros((head_count, count_query, DH), jnp.float32),
            )
        )
    states = tuple(initial)
    key_offset = jnp.int32(0)
    key_whole = lax.all_gather(keys, "ctx", axis=0, tiled=True)
    value_whole = lax.all_gather(values, "ctx", axis=0, tiled=True)
    total_keys = key_whole.shape[0]
    step_rows = min(total_keys, 1024)
    for begin in range(0, total_keys, step_rows):
        key_block = key_whole[begin : begin + step_rows]
        value_block = value_whole[begin : begin + step_rows]
        block_offset = key_offset + begin
        query_rows, query_offset = query_sets[0]
        needed = block_offset <= query_offset + query_rows.shape[0] - 1
        updated = [
            lax.cond(
                needed,
                lambda carried, rows_now=query_rows, offset_now=query_offset, keys_now=key_block, values_now=value_block, start_now=block_offset: update_state(
                    carried, rows_now, offset_now, keys_now, values_now, start_now
                ),
                lambda carried: carried,
                states[0],
            )
        ]
        states = tuple(updated)
    results = []
    for maxima, totals, numer in states:
        result = (numer / totals[..., None]).astype(jnp.bfloat16)
        results.append(
            jnp.transpose(result, (1, 0, 2)).reshape(result.shape[1], result.shape[0] * DH)
        )
    return results


def body(
    queries,
    keys,
    values,
    resid,
    out_proj,
    norm_gain,
    up_proj,
    down_proj,
    router,
    expert_ids,
    expert_in,
    expert_out,
):
    tok_rows = queries.shape[0]
    width = resid.shape[1]
    live_count = router.shape[1]
    ctx_count = lax.axis_size("ctx")
    device_index = lax.axis_index("ctx")
    base_offset = device_index * tok_rows
    attn = attend([(queries, base_offset)], keys, values)[0]
    mixed = resid.astype(jnp.float32) + jnp.dot(attn, out_proj, preferred_element_type=jnp.float32)
    normed = (
        mixed * lax.rsqrt(jnp.mean(mixed * mixed, axis=1, keepdims=True) + EPSILON) * norm_gain
    ).astype(jnp.bfloat16)
    mlp_blocks = jnp.stack([up_proj, down_proj], 0)
    for level in range(live_count.bit_length() - 1):
        other_block = from_partner(mlp_blocks, "ctx", level)
        mlp_blocks = jnp.concatenate([mlp_blocks, other_block], axis=2)
    slots_per = max(2, 5 * tok_rows // (4 * live_count))
    chosen = expert_ids[:, 0]
    onehot = (chosen[:, None] == jnp.arange(live_count, dtype=jnp.int32)[None, :]).astype(
        jnp.bfloat16
    )
    row_iota = jnp.arange(tok_rows, dtype=jnp.int32)
    strictly_lower = (row_iota[None, :] < row_iota[:, None]).astype(jnp.bfloat16)
    counts_before = jnp.dot(strictly_lower, onehot, preferred_element_type=jnp.float32)
    slot_index = jnp.sum(onehot.astype(jnp.float32) * counts_before, axis=1).astype(jnp.int32)
    target_slot = chosen * slots_per + slot_index
    dispatch_matrix = (
        jnp.arange(live_count * slots_per, dtype=jnp.int32)[:, None] == target_slot[None, :]
    ).astype(jnp.bfloat16)
    packed = jnp.dot(dispatch_matrix, normed, preferred_element_type=jnp.float32).astype(
        jnp.bfloat16
    )
    sending = jnp.broadcast_to(
        packed.reshape(1, live_count, slots_per, width), (SPLIT, live_count, slots_per, width)
    )
    sending = sending.reshape(ctx_count, 1, slots_per, width)
    own_expert = device_index % live_count
    router_column = lax.dynamic_slice_in_dim(router, own_expert, 1, 1)
    weight_in = expert_in[0]
    weight_out = expert_out[0]
    received = lax.all_to_all(sending, "ctx", split_axis=0, concat_axis=1, tiled=True)
    rows = received.reshape(-1, width)
    expert_hidden = jax.nn.gelu(
        jnp.dot(rows, weight_in, preferred_element_type=jnp.float32)
    ).astype(jnp.bfloat16)
    mlp_hidden = jax.nn.gelu(
        jnp.dot(rows, mlp_blocks[0], preferred_element_type=jnp.float32)
    ).astype(jnp.bfloat16)
    gate = jax.nn.sigmoid(jnp.dot(rows, router_column, preferred_element_type=jnp.float32))
    produced = gate * jnp.dot(expert_hidden, weight_out, preferred_element_type=jnp.float32)
    produced = produced + lax.dot_general(
        mlp_hidden, mlp_blocks[1], (((1,), (1,)), ((), ())), preferred_element_type=jnp.float32
    )
    came_back = lax.all_to_all(
        produced.astype(jnp.bfloat16).reshape(received.shape),
        "ctx",
        split_axis=1,
        concat_axis=0,
        tiled=True,
    )
    summed = jnp.sum(
        came_back.astype(jnp.float32).reshape(SPLIT, live_count * slots_per, width), axis=0
    )
    mixture_part = lax.dot_general(
        dispatch_matrix.astype(jnp.float32),
        summed,
        (((0,), (0,)), ((), ())),
        precision=lax.Precision.HIGHEST,
        preferred_element_type=jnp.float32,
    )
    return (mixed + mixture_part).astype(jnp.bfloat16)


LOG2_E = 1.4426950408889634


def swap(array, mask, among=lambda at: True):
    pairs = [(i, i ^ mask) for i in range(lax.axis_size("ctx")) if among(i)]
    return lax.ppermute(array, "ctx", pairs)


VMEM = pl.BlockSpec(memory_space=pltpu.VMEM)
SMEM = pl.BlockSpec(memory_space=pltpu.SMEM)


HBM = pl.BlockSpec(memory_space=pltpu.HBM)


def call(kernel, outs, specs, flops, mib, *operands, copies=0, scratch=()):
    return pl.pallas_call(
        kernel,
        out_shape=outs,
        in_specs=specs,
        out_specs=[VMEM] * len(outs),
        scratch_shapes=[*scratch] + ([pltpu.SemaphoreType.DMA((copies,))] if copies else []),
        compiler_params=pltpu.CompilerParams(vmem_limit_bytes=mib * 2**20),
        cost_estimate=pl.CostEstimate(
            flops=flops,
            bytes_accessed=sum(x.size * x.dtype.itemsize for x in operands),
            transcendentals=0,
        ),
    )(*operands)


def copy_all(pairs, sems):
    copies = [pltpu.make_async_copy(a, b, sems.at[at]) for at, (a, b) in enumerate(pairs)]
    for copy in copies:
        copy.start()
    for copy in copies:
        copy.wait()


def load_kernel(*refs):
    count = len(refs) // 2
    copy_all(zip(refs[:count], refs[count : 2 * count]), refs[-1])


def load(mib, *arrays):
    outs = [pltpu.VMEM(array.shape, array.dtype) for array in arrays]
    count = len(arrays)
    return call(load_kernel, outs, [HBM] * count, 0, mib, *arrays, copies=count)


def pack_kernel(index_ref, query_ref, key_ref, value_ref, *refs):
    pairs = []
    for at, out_ref in enumerate(refs[:-1]):
        head = (index_ref[0] ^ 2 * at) >> 1
        columns = pl.ds(pl.multiple_of(head * DH, DH), DH)
        for part, ref in enumerate((query_ref, key_ref, value_ref)):
            pairs.append((ref.at[:, columns], out_ref.at[:, pl.ds(part * DH, DH)]))
    copy_all(pairs, refs[-1])


def arrange_kernel(index_ref, *refs):
    query_ref, pair_ref = refs[-2:]
    for at, ref in enumerate(refs[:-2]):
        place = (index_ref[0] ^ 2 * at) >> 1
        query_ref[place] = ref[:, :DH]
        pair_ref[place] = ref[:, DH:]


def attention_kernel(index_ref, query_ref, own_ref, other_ref, ids_ref, *refs):
    out_refs, (held, ids, sem) = refs[:-3], refs[-3:]
    ids_copy = pltpu.make_async_copy(ids_ref, ids, sem.at[0])
    ids_copy.start()
    blocks, rows, _ = own_ref.shape
    row_at = lax.broadcasted_iota(jnp.int32, (rows, rows), 0)
    column_at = lax.broadcasted_iota(jnp.int32, (rows, rows), 1)
    causal = column_at <= row_at
    also = jnp.broadcast_to(index_ref[0] & 1 == 1, (rows, rows))
    contract = (((1,), (1,)), ((), ()))
    for block in range(blocks):
        query = query_ref[block]
        pair = []
        for ref, last_visible in ((own_ref, causal), (other_ref, also)):
            seen = ref[: block + 1].reshape((block + 1) * rows, 2 * DH)
            score = lax.dot_general(
                query, seen[:, :DH], contract, preferred_element_type=jnp.float32
            )
            last = jnp.where(last_visible, score[:, block * rows :], NEG_FILL)
            if block:
                score = jnp.concatenate([score[:, : block * rows], last], axis=1)
            else:
                score = last
            pair.append((score, seen[:, DH:]))
        row_max = jnp.maximum(
            *(jnp.max(score, axis=1, keepdims=True) for score, _ in pair)
        )
        numer, totals = 0.0, 0.0
        for score, value in pair:
            weights = jnp.exp2((score - row_max) * (DH ** (-0.5) * LOG2_E))
            totals = totals + jnp.sum(weights, axis=1, keepdims=True)
            numer = numer + jnp.dot(
                weights.astype(jnp.bfloat16), value, preferred_element_type=jnp.float32
            )
        held[block] = (numer / totals).astype(jnp.bfloat16)
    ids_copy.wait()
    id_rows = jnp.broadcast_to(
        ids[...].astype(jnp.float32), (out_refs[0].shape[0] - rows, rows)
    ).astype(jnp.bfloat16)
    for at, out_ref in enumerate(out_refs):
        out_ref[:rows, :] = held[(index_ref[0] ^ 2 * at) >> 1]
        out_ref[rows:, :] = id_rows


def project_kernel(index_ref, weight_ref, resid_ref, gain_ref, *refs):
    heads_in, (mixed_ref, normed_ref, top_ref, bottom_ref, held) = refs[:-5], refs[-5:]
    rows = resid_ref.shape[0]
    for at, ref in enumerate(heads_in):
        held[(index_ref[0] ^ 2 * at) >> 1] = ref[:rows, :]
    attn = jnp.concatenate([held[head] for head in range(len(heads_in))], axis=1)
    mixed = resid_ref[...].astype(jnp.float32) + jnp.dot(
        attn, weight_ref[...], preferred_element_type=jnp.float32
    )
    mixed_ref[...] = mixed
    scale = lax.rsqrt(jnp.mean(mixed * mixed, axis=1, keepdims=True) + EPSILON)
    normed = (mixed * scale * gain_ref[...]).astype(jnp.bfloat16)
    normed_ref[...] = normed
    top_ref[...] = normed[: rows // 2]
    bottom_ref[...] = normed[rows // 2 :]


def mixture_kernel(
    start, index_ref, router_ref, up_a, up_b, in_a, in_b, down_a, down_b, out_a, out_b, *refs
):
    count = len(refs) // 3
    shards, ids_refs, out_refs = refs[:count], refs[count : 2 * count], refs[2 * count :]
    rows, width = shards[0].shape
    own = (index_ref[0] & 1).astype(jnp.float32)

    def expert(ref):
        count = ref.shape[1]
        ids = ref[count : count + 16, :].astype(jnp.float32)[0:1, :]
        column = jnp.transpose(jnp.broadcast_to(ids, (count, count)))[:, 0:1]
        return column[start : start + rows]

    normed = jnp.concatenate([ref[...] for ref in shards], axis=0)
    chosen = jnp.concatenate([expert(ref) for ref in ids_refs], axis=0)
    mine = chosen == own
    router = router_ref[...].astype(jnp.float32)
    column = jnp.where(chosen > 0, router[1:2, :], router[0:1, :])
    logits = jnp.sum(normed.astype(jnp.float32) * column, axis=1, keepdims=True)
    gate = jax.nn.sigmoid(logits)

    def hidden(weights):
        return jax.nn.gelu(jnp.dot(normed, weights[...], preferred_element_type=jnp.float32))

    mlp_a = hidden(up_a).astype(jnp.bfloat16)
    mlp_b = hidden(up_b).astype(jnp.bfloat16)
    exp_a = jnp.where(mine, hidden(in_a), 0.0).astype(jnp.bfloat16)
    exp_b = jnp.where(mine, 0.0, hidden(in_b)).astype(jnp.bfloat16)
    contract = (((1,), (1,)), ((), ()))
    step = min(width, 512)
    for begin in range(0, width, step):
        span = slice(begin, begin + step)
        part = gate * (
            jnp.dot(exp_a, out_a[:, span], preferred_element_type=jnp.float32)
            + jnp.dot(exp_b, out_b[:, span], preferred_element_type=jnp.float32)
        )
        part = part + (
            lax.dot_general(mlp_a, down_a[span, :], contract, preferred_element_type=jnp.float32)
            + lax.dot_general(mlp_b, down_b[span, :], contract, preferred_element_type=jnp.float32)
        )
        part = part.astype(jnp.bfloat16)
        for at, out_ref in enumerate(out_refs):
            out_ref[:, span] = part[at * rows : (at + 1) * rows]


def finish_kernel(mixed_ref, *refs):
    whole, split, out_ref = refs[:3], refs[3:-1], refs[-1]
    rows = mixed_ref.shape[0]
    for at in range(2):
        span = slice(at * rows // 2, (at + 1) * rows // 2)
        total = mixed_ref[span, :]
        for ref in whole:
            total = total + ref[span, :].astype(jnp.float32)
        for ref in split[at::2]:
            total = total + ref[...].astype(jnp.float32)
        out_ref[span, :] = total.astype(jnp.bfloat16)


def body_by_pairs(
    queries,
    keys,
    values,
    resid,
    out_proj,
    norm_gain,
    up_proj,
    down_proj,
    router,
    expert_ids,
    expert_in,
    expert_out,
):
    rows, width = resid.shape
    heads = queries.shape[1] // DH
    device_index = lax.axis_index("ctx")
    index = device_index.reshape(1)
    shape = jax.ShapeDtypeStruct
    packed = call(
        pack_kernel,
        [pltpu.VMEM((rows, 3 * DH), jnp.bfloat16)] * heads,
        [SMEM] + [HBM] * 3,
        0,
        62,
        index,
        queries,
        keys,
        values,
        copies=3 * heads,
    )
    blocks = [packed[0]] + [swap(packed[at], 2 * at) for at in range(1, heads)]
    query, own = call(
        arrange_kernel,
        [shape((heads, rows, DH), jnp.bfloat16), shape((heads, rows, 2 * DH), jnp.bfloat16)],
        [SMEM] + [VMEM] * heads,
        0,
        8,
        index,
        *blocks,
    )
    other = swap(own, 1)
    weights_own = (up_proj, expert_in[0], down_proj, expert_out[0])
    weights_other = [swap(array, 1) for array in weights_own]
    *weights_own, out_weight, resid_rows = load(44, *weights_own, out_proj, resid)
    weights = tuple(w for pair in zip(weights_own, weights_other) for w in pair)
    outs = call(
        attention_kernel,
        [pltpu.VMEM((rows + 16, DH), jnp.bfloat16)] * heads,
        [SMEM] + [VMEM] * 3 + [HBM],
        10**9,
        12,
        index,
        query,
        own,
        other,
        expert_ids.reshape(1, rows),
        copies=1,
        scratch=[pltpu.VMEM((heads, rows, DH), jnp.bfloat16), pltpu.VMEM((1, rows), jnp.int32)],
    )
    backs = [outs[0]] + [swap(outs[at], 2 * at) for at in range(1, heads)]
    mixed, normed, *halves = call(
        project_kernel,
        [pltpu.VMEM((rows, width), jnp.float32), pltpu.VMEM((rows, width), jnp.bfloat16)]
        + [pltpu.VMEM((rows // 2, width), jnp.bfloat16)] * 2,
        [SMEM] + [VMEM] * (heads + 3),
        2 * out_proj.size * rows,
        12,
        index,
        out_weight,
        resid_rows,
        norm_gain.reshape(1, width),
        *backs,
        scratch=[pltpu.VMEM((heads, rows, DH), jnp.bfloat16)],
    )
    units = sum(w.size for w in weights[:4]) // width

    def mix(shards, start=0):
        count = next(iter(shards.values())).shape[0]
        return call(
            functools.partial(mixture_kernel, start),
            [pltpu.VMEM((count, width), jnp.bfloat16)] * len(shards),
            [SMEM] + [VMEM] * (9 + 2 * len(shards)),
            4 * len(shards) * count * width * units,
            16,
            index,
            router.T,
            *weights,
            *shards.values(),
            *(backs[offset // 2] for offset in shards),
        )

    def plus(*terms):
        return sum(term.astype(jnp.float32) for term in terms).astype(jnp.bfloat16)

    def inner(at):
        return (at >> 2 ^ at >> 3) & 1 == 1

    def outer(at):
        return not inner(at)

    across = swap(normed, 2)
    beside = swap(normed, 4)
    beside_across = swap(across, 4)
    arrived, passed = [], {}
    for offset in (12, 8):
        for half, rows_sent in zip("ab", halves):
            first = swap(rows_sent, offset)
            second = swap(first, 2)
            start = 0 if half == "a" else rows // 2
            part, part_across = mix({offset: first, offset | 2: second}, start)
            returned = swap(part_across, 2)
            if offset == 12:
                summed = plus(part, returned)
                arrived.append(swap(summed, 12, inner))
                passed[half] = swap(summed, 4, outer)
            else:
                summed = plus(part, returned, passed[half])
                arrived.append(swap(summed, 8))
    part, part_across = mix({0: normed, 2: across})
    (part_beside,) = mix({4: beside})
    (part_both,) = mix({6: beside_across})
    summed = plus(part_across, swap(part_both, 4))
    (result,) = call(
        finish_kernel,
        [shape((rows, width), jnp.bfloat16)],
        [VMEM] * (4 + len(arrived)),
        0,
        12,
        mixed,
        part,
        swap(part_beside, 4),
        swap(summed, 2),
        *arrived,
    )
    return result


def solution(mesh):
    ctx_count = mesh.shape["ctx"]

    def by_pairs(args):
        queries, router = args[0], args[8]
        return (
            router.shape[1] == 2
            and ctx_count == 2 * SPLIT
            and queries.shape[1] == ctx_count // 2 * DH
            and ctx_count == 16
        )

    def chosen(*args):
        if not by_pairs(args):
            return body(*args)
        return body_by_pairs(*args)

    placed = (
        P(("groups", "ctx"), None),
        P(("groups", "ctx"), None),
        P(("groups", "ctx"), None),
        P(("groups", "ctx"), None),
        P(),
        P(),
        P(None, "ctx"),
        P(None, "ctx"),
        P(),
        P(("groups", "ctx"), None),
        P("ctx", None, None),
        P("ctx", None, None),
    )
    return jax.shard_map(
        chosen, mesh=mesh, in_specs=placed, out_specs=P(("groups", "ctx"), None), check_vma=False
    )
```

```python
import functools
import jax
import jax.numpy as jnp
from jax import lax
from jax.experimental import pallas as pl
from jax.experimental.pallas import tpu as pltpu
from jax.sharding import PartitionSpec as P

DH = 128
SPLIT = 8


NEG_FILL = -1e30
EPSILON = 1e-06


def from_partner(array, axis, apart):
    return lax.ppermute(array, axis, [(i, i ^ 1 << apart) for i in range(lax.axis_size(axis))])


def update_state(state, query_rows, query_offset, key_block, value_block, key_offset):
    maxima, totals, numer = state
    count_query = query_rows.shape[0]
    count_keys = key_block.shape[0]
    head_count = query_rows.shape[1] // DH
    query_heads = query_rows.reshape(count_query, head_count, DH)
    key_heads = key_block.reshape(count_keys, head_count, DH)
    value_heads = value_block.reshape(count_keys, head_count, DH)
    scores = jnp.einsum(
        "qhd,khd->hqk", query_heads, key_heads, preferred_element_type=jnp.float32
    ) * DH ** (-0.5)
    query_positions = query_offset + jnp.arange(count_query, dtype=jnp.int32)
    key_positions = key_offset + jnp.arange(count_keys, dtype=jnp.int32)
    visible = (key_positions[None, :] <= query_positions[:, None])[None]
    masked = jnp.where(visible, scores, NEG_FILL)
    new_max = jnp.maximum(maxima, jnp.max(masked, axis=2))
    weights = jnp.where(visible, jnp.exp(masked - new_max[..., None]), 0.0)
    factor = jnp.exp(maxima - new_max)
    totals = totals * factor + jnp.sum(weights, axis=2)
    numer = numer * factor[..., None] + jnp.einsum(
        "hqk,khd->hqd",
        weights.astype(jnp.bfloat16),
        value_heads,
        preferred_element_type=jnp.float32,
    )
    return (new_max, totals, numer)


def attend(query_sets, keys, values):
    head_count = keys.shape[1] // DH
    initial = []
    for query_rows, query_offset in query_sets:
        count_query = query_rows.shape[0]
        initial.append(
            (
                jnp.full((head_count, count_query), NEG_FILL, jnp.float32),
                jnp.zeros((head_count, count_query), jnp.float32),
                jnp.zeros((head_count, count_query, DH), jnp.float32),
            )
        )
    states = tuple(initial)
    key_offset = jnp.int32(0)
    key_whole = lax.all_gather(keys, "ctx", axis=0, tiled=True)
    value_whole = lax.all_gather(values, "ctx", axis=0, tiled=True)
    total_keys = key_whole.shape[0]
    step_rows = min(total_keys, 1024)
    for begin in range(0, total_keys, step_rows):
        key_block = key_whole[begin : begin + step_rows]
        value_block = value_whole[begin : begin + step_rows]
        block_offset = key_offset + begin
        query_rows, query_offset = query_sets[0]
        needed = block_offset <= query_offset + query_rows.shape[0] - 1
        updated = [
            lax.cond(
                needed,
                lambda carried, rows_now=query_rows, offset_now=query_offset, keys_now=key_block, values_now=value_block, start_now=block_offset: update_state(
                    carried, rows_now, offset_now, keys_now, values_now, start_now
                ),
                lambda carried: carried,
                states[0],
            )
        ]
        states = tuple(updated)
    results = []
    for maxima, totals, numer in states:
        result = (numer / totals[..., None]).astype(jnp.bfloat16)
        results.append(
            jnp.transpose(result, (1, 0, 2)).reshape(result.shape[1], result.shape[0] * DH)
        )
    return results


def body(
    queries,
    keys,
    values,
    resid,
    out_proj,
    norm_gain,
    up_proj,
    down_proj,
    router,
    expert_ids,
    expert_in,
    expert_out,
):
    tok_rows = queries.shape[0]
    width = resid.shape[1]
    live_count = router.shape[1]
    ctx_count = lax.axis_size("ctx")
    device_index = lax.axis_index("ctx")
    base_offset = device_index * tok_rows
    attn = attend([(queries, base_offset)], keys, values)[0]
    mixed = resid.astype(jnp.float32) + jnp.dot(attn, out_proj, preferred_element_type=jnp.float32)
    normed = (
        mixed * lax.rsqrt(jnp.mean(mixed * mixed, axis=1, keepdims=True) + EPSILON) * norm_gain
    ).astype(jnp.bfloat16)
    mlp_blocks = jnp.stack([up_proj, down_proj], 0)
    for level in range(live_count.bit_length() - 1):
        other_block = from_partner(mlp_blocks, "ctx", level)
        mlp_blocks = jnp.concatenate([mlp_blocks, other_block], axis=2)
    slots_per = max(2, 5 * tok_rows // (4 * live_count))
    chosen = expert_ids[:, 0]
    onehot = (chosen[:, None] == jnp.arange(live_count, dtype=jnp.int32)[None, :]).astype(
        jnp.bfloat16
    )
    row_iota = jnp.arange(tok_rows, dtype=jnp.int32)
    strictly_lower = (row_iota[None, :] < row_iota[:, None]).astype(jnp.bfloat16)
    counts_before = jnp.dot(strictly_lower, onehot, preferred_element_type=jnp.float32)
    slot_index = jnp.sum(onehot.astype(jnp.float32) * counts_before, axis=1).astype(jnp.int32)
    target_slot = chosen * slots_per + slot_index
    dispatch_matrix = (
        jnp.arange(live_count * slots_per, dtype=jnp.int32)[:, None] == target_slot[None, :]
    ).astype(jnp.bfloat16)
    packed = jnp.dot(dispatch_matrix, normed, preferred_element_type=jnp.float32).astype(
        jnp.bfloat16
    )
    sending = jnp.broadcast_to(
        packed.reshape(1, live_count, slots_per, width), (SPLIT, live_count, slots_per, width)
    )
    sending = sending.reshape(ctx_count, 1, slots_per, width)
    own_expert = device_index % live_count
    router_column = lax.dynamic_slice_in_dim(router, own_expert, 1, 1)
    weight_in = expert_in[0]
    weight_out = expert_out[0]
    received = lax.all_to_all(sending, "ctx", split_axis=0, concat_axis=1, tiled=True)
    rows = received.reshape(-1, width)
    expert_hidden = jax.nn.gelu(
        jnp.dot(rows, weight_in, preferred_element_type=jnp.float32)
    ).astype(jnp.bfloat16)
    mlp_hidden = jax.nn.gelu(
        jnp.dot(rows, mlp_blocks[0], preferred_element_type=jnp.float32)
    ).astype(jnp.bfloat16)
    gate = jax.nn.sigmoid(jnp.dot(rows, router_column, preferred_element_type=jnp.float32))
    produced = gate * jnp.dot(expert_hidden, weight_out, preferred_element_type=jnp.float32)
    produced = produced + lax.dot_general(
        mlp_hidden, mlp_blocks[1], (((1,), (1,)), ((), ())), preferred_element_type=jnp.float32
    )
    came_back = lax.all_to_all(
        produced.astype(jnp.bfloat16).reshape(received.shape),
        "ctx",
        split_axis=1,
        concat_axis=0,
        tiled=True,
    )
    summed = jnp.sum(
        came_back.astype(jnp.float32).reshape(SPLIT, live_count * slots_per, width), axis=0
    )
    mixture_part = lax.dot_general(
        dispatch_matrix.astype(jnp.float32),
        summed,
        (((0,), (0,)), ((), ())),
        precision=lax.Precision.HIGHEST,
        preferred_element_type=jnp.float32,
    )
    return (mixed + mixture_part).astype(jnp.bfloat16)


LOG2_E = 1.4426950408889634


def swap(array, mask, among=lambda at: True):
    pairs = [(i, i ^ mask) for i in range(lax.axis_size("ctx")) if among(i)]
    return lax.ppermute(array, "ctx", pairs)


VMEM = pl.BlockSpec(memory_space=pltpu.VMEM)
SMEM = pl.BlockSpec(memory_space=pltpu.SMEM)


HBM = pl.BlockSpec(memory_space=pltpu.HBM)


def call(kernel, outs, specs, flops, mib, *operands, copies=0, scratch=()):
    return pl.pallas_call(
        kernel,
        out_shape=outs,
        in_specs=specs,
        out_specs=[VMEM] * len(outs),
        scratch_shapes=[*scratch] + ([pltpu.SemaphoreType.DMA((copies,))] if copies else []),
        compiler_params=pltpu.CompilerParams(vmem_limit_bytes=mib * 2**20),
        cost_estimate=pl.CostEstimate(
            flops=flops,
            bytes_accessed=sum(x.size * x.dtype.itemsize for x in operands),
            transcendentals=0,
        ),
    )(*operands)


def copy_all(pairs, sems):
    copies = [pltpu.make_async_copy(a, b, sems.at[at]) for at, (a, b) in enumerate(pairs)]
    for copy in copies:
        copy.start()
    for copy in copies:
        copy.wait()


def load_kernel(*refs):
    count = len(refs) // 2
    copy_all(zip(refs[:count], refs[count : 2 * count]), refs[-1])


def load(mib, *arrays):
    outs = [pltpu.VMEM(array.shape, array.dtype) for array in arrays]
    count = len(arrays)
    return call(load_kernel, outs, [HBM] * count, 0, mib, *arrays, copies=count)


def pack_kernel(index_ref, query_ref, key_ref, value_ref, *refs):
    pairs = []
    for at, out_ref in enumerate(refs[:-1]):
        head = (index_ref[0] ^ 2 * at) >> 1
        columns = pl.ds(pl.multiple_of(head * DH, DH), DH)
        for part, ref in enumerate((query_ref, key_ref, value_ref)):
            pairs.append((ref.at[:, columns], out_ref.at[:, pl.ds(part * DH, DH)]))
    copy_all(pairs, refs[-1])


def arrange_kernel(index_ref, *refs):
    query_ref, pair_ref = refs[-2:]
    for at, ref in enumerate(refs[:-2]):
        place = (index_ref[0] ^ 2 * at) >> 1
        query_ref[place] = ref[:, :DH]
        pair_ref[place] = ref[:, DH:]


def attention_kernel(index_ref, query_ref, own_ref, other_ref, ids_ref, *refs):
    out_refs, (held, ids, sem) = refs[:-3], refs[-3:]
    ids_copy = pltpu.make_async_copy(ids_ref, ids, sem.at[0])
    ids_copy.start()
    blocks, rows, _ = own_ref.shape
    row_at = lax.broadcasted_iota(jnp.int32, (rows, rows), 0)
    column_at = lax.broadcasted_iota(jnp.int32, (rows, rows), 1)
    causal = column_at <= row_at
    also = jnp.broadcast_to(index_ref[0] & 1 == 1, (rows, rows))
    contract = (((1,), (1,)), ((), ()))
    for block in range(blocks):
        query = query_ref[block]
        pair = []
        for ref, last_visible in ((own_ref, causal), (other_ref, also)):
            seen = ref[: block + 1].reshape((block + 1) * rows, 2 * DH)
            score = lax.dot_general(
                query, seen[:, :DH], contract, preferred_element_type=jnp.float32
            )
            last = jnp.where(last_visible, score[:, block * rows :], NEG_FILL)
            if block:
                score = jnp.concatenate([score[:, : block * rows], last], axis=1)
            else:
                score = last
            pair.append((score, seen[:, DH:]))
        row_max = jnp.maximum(
            *(jnp.max(score, axis=1, keepdims=True) for score, _ in pair)
        )
        numer, totals = 0.0, 0.0
        for score, value in pair:
            weights = jnp.exp2((score - row_max) * (DH ** (-0.5) * LOG2_E))
            totals = totals + jnp.sum(weights, axis=1, keepdims=True)
            numer = numer + jnp.dot(
                weights.astype(jnp.bfloat16), value, preferred_element_type=jnp.float32
            )
        held[block] = (numer / totals).astype(jnp.bfloat16)
    ids_copy.wait()
    id_rows = jnp.broadcast_to(
        ids[...].astype(jnp.float32), (out_refs[0].shape[0] - rows, rows)
    ).astype(jnp.bfloat16)
    for at, out_ref in enumerate(out_refs):
        out_ref[:rows, :] = held[(index_ref[0] ^ 2 * at) >> 1]
        out_ref[rows:, :] = id_rows


def project_kernel(index_ref, weight_ref, resid_ref, gain_ref, *refs):
    heads_in, (mixed_ref, normed_ref, top_ref, bottom_ref, held) = refs[:-5], refs[-5:]
    rows = resid_ref.shape[0]
    for at, ref in enumerate(heads_in):
        held[(index_ref[0] ^ 2 * at) >> 1] = ref[:rows, :]
    attn = jnp.concatenate([held[head] for head in range(len(heads_in))], axis=1)
    mixed = resid_ref[...].astype(jnp.float32) + jnp.dot(
        attn, weight_ref[...], preferred_element_type=jnp.float32
    )
    mixed_ref[...] = mixed
    scale = lax.rsqrt(jnp.mean(mixed * mixed, axis=1, keepdims=True) + EPSILON)
    normed = (mixed * scale * gain_ref[...]).astype(jnp.bfloat16)
    normed_ref[...] = normed
    top_ref[...] = normed[: rows // 2]
    bottom_ref[...] = normed[rows // 2 :]


def mixture_kernel(
    start, index_ref, router_ref, up_a, up_b, in_a, in_b, down_a, down_b, out_a, out_b, *refs
):
    count = len(refs) // 3
    shards, ids_refs, out_refs = refs[:count], refs[count : 2 * count], refs[2 * count :]
    rows, width = shards[0].shape
    own = (index_ref[0] & 1).astype(jnp.float32)

    def expert(ref):
        count = ref.shape[1]
        ids = ref[count : count + 16, :].astype(jnp.float32)[0:1, :]
        column = jnp.transpose(jnp.broadcast_to(ids, (count, count)))[:, 0:1]
        return column[start : start + rows]

    normed = jnp.concatenate([ref[...] for ref in shards], axis=0)
    chosen = jnp.concatenate([expert(ref) for ref in ids_refs], axis=0)
    mine = chosen == own
    router = router_ref[...].astype(jnp.float32)
    column = jnp.where(chosen > 0, router[1:2, :], router[0:1, :])
    logits = jnp.sum(normed.astype(jnp.float32) * column, axis=1, keepdims=True)
    gate = jax.nn.sigmoid(logits)

    def hidden(weights):
        return jax.nn.gelu(jnp.dot(normed, weights[...], preferred_element_type=jnp.float32))

    mlp_a = hidden(up_a).astype(jnp.bfloat16)
    mlp_b = hidden(up_b).astype(jnp.bfloat16)
    exp_a = jnp.where(mine, hidden(in_a), 0.0).astype(jnp.bfloat16)
    exp_b = jnp.where(mine, 0.0, hidden(in_b)).astype(jnp.bfloat16)
    contract = (((1,), (1,)), ((), ()))
    step = min(width, 512)
    for begin in range(0, width, step):
        span = slice(begin, begin + step)
        part = gate * (
            jnp.dot(exp_a, out_a[:, span], preferred_element_type=jnp.float32)
            + jnp.dot(exp_b, out_b[:, span], preferred_element_type=jnp.float32)
        )
        part = part + (
            lax.dot_general(mlp_a, down_a[span, :], contract, preferred_element_type=jnp.float32)
            + lax.dot_general(mlp_b, down_b[span, :], contract, preferred_element_type=jnp.float32)
        )
        part = part.astype(jnp.bfloat16)
        for at, out_ref in enumerate(out_refs):
            out_ref[:, span] = part[at * rows : (at + 1) * rows]


def finish_kernel(mixed_ref, *refs):
    whole, split, out_ref = refs[:3], refs[3:-1], refs[-1]
    rows = mixed_ref.shape[0]
    for at in range(2):
        span = slice(at * rows // 2, (at + 1) * rows // 2)
        total = mixed_ref[span, :]
        for ref in whole:
            total = total + ref[span, :].astype(jnp.float32)
        for ref in split[at::2]:
            total = total + ref[...].astype(jnp.float32)
        out_ref[span, :] = total.astype(jnp.bfloat16)


def body_by_pairs(
    queries,
    keys,
    values,
    resid,
    out_proj,
    norm_gain,
    up_proj,
    down_proj,
    router,
    expert_ids,
    expert_in,
    expert_out,
):
    rows, width = resid.shape
    heads = queries.shape[1] // DH
    device_index = lax.axis_index("ctx")
    index = device_index.reshape(1)
    shape = jax.ShapeDtypeStruct
    packed = call(
        pack_kernel,
        [pltpu.VMEM((rows, 3 * DH), jnp.bfloat16)] * heads,
        [SMEM] + [HBM] * 3,
        0,
        62,
        index,
        queries,
        keys,
        values,
        copies=3 * heads,
    )
    blocks = [packed[0]] + [swap(packed[at], 2 * at) for at in range(1, heads)]
    query, own = call(
        arrange_kernel,
        [shape((heads, rows, DH), jnp.bfloat16), shape((heads, rows, 2 * DH), jnp.bfloat16)],
        [SMEM] + [VMEM] * heads,
        0,
        8,
        index,
        *blocks,
    )
    other = swap(own, 1)
    weights_own = (up_proj, expert_in[0], down_proj, expert_out[0])
    weights_other = [swap(array, 1) for array in weights_own]
    *weights_own, out_weight, resid_rows = load(44, *weights_own, out_proj, resid)
    weights = tuple(w for pair in zip(weights_own, weights_other) for w in pair)
    outs = call(
        attention_kernel,
        [pltpu.VMEM((rows + 16, DH), jnp.bfloat16)] * heads,
        [SMEM] + [VMEM] * 3 + [HBM],
        10**9,
        12,
        index,
        query,
        own,
        other,
        expert_ids.reshape(1, rows),
        copies=1,
        scratch=[pltpu.VMEM((heads, rows, DH), jnp.bfloat16), pltpu.VMEM((1, rows), jnp.int32)],
    )
    backs = [outs[0]] + [swap(outs[at], 2 * at) for at in range(1, heads)]
    mixed, normed, *halves = call(
        project_kernel,
        [pltpu.VMEM((rows, width), jnp.float32), pltpu.VMEM((rows, width), jnp.bfloat16)]
        + [pltpu.VMEM((rows // 2, width), jnp.bfloat16)] * 2,
        [SMEM] + [VMEM] * (heads + 3),
        2 * out_proj.size * rows,
        12,
        index,
        out_weight,
        resid_rows,
        norm_gain.reshape(1, width),
        *backs,
        scratch=[pltpu.VMEM((heads, rows, DH), jnp.bfloat16)],
    )
    units = sum(w.size for w in weights[:4]) // width

    def mix(shards, start=0):
        count = next(iter(shards.values())).shape[0]
        return call(
            functools.partial(mixture_kernel, start),
            [pltpu.VMEM((count, width), jnp.bfloat16)] * len(shards),
            [SMEM] + [VMEM] * (9 + 2 * len(shards)),
            4 * len(shards) * count * width * units,
            16,
            index,
            router.T,
            *weights,
            *shards.values(),
            *(backs[offset // 2] for offset in shards),
        )

    def plus(*terms):
        return sum(term.astype(jnp.float32) for term in terms).astype(jnp.bfloat16)

    def inner(at):
        return (at >> 2 ^ at >> 3) & 1 == 1

    def outer(at):
        return not inner(at)

    across = swap(normed, 2)
    beside = swap(normed, 4)
    beside_across = swap(across, 4)
    arrived, passed = [], {}
    for offset in (12, 8):
        for half, rows_sent in zip("ab", halves):
            name = f"{offset}{half}"
            first = swap(rows_sent, offset)
            second = swap(first, 2)
            start = 0 if half == "a" else rows // 2
            part, part_across = mix({offset: first, offset | 2: second}, start)
            returned = swap(part_across, 2)
            summed = plus(part, returned, *passed.get(name, ()))
            if name == "12b":
                arrived.append(swap(summed, 12, inner))
                passed["8b"] = [swap(summed, 4, outer)]
            else:
                arrived.append(swap(summed, offset))
    part, part_across = mix({0: normed, 2: across})
    (part_beside,) = mix({4: beside})
    (part_both,) = mix({6: beside_across})
    summed = plus(part_across, swap(part_both, 4))
    (result,) = call(
        finish_kernel,
        [shape((rows, width), jnp.bfloat16)],
        [VMEM] * (4 + len(arrived)),
        0,
        12,
        mixed,
        part,
        swap(part_beside, 4),
        swap(summed, 2),
        *arrived,
    )
    return result


def solution(mesh):
    ctx_count = mesh.shape["ctx"]

    def by_pairs(args):
        queries, router = args[0], args[8]
        return (
            router.shape[1] == 2
            and ctx_count == 2 * SPLIT
            and queries.shape[1] == ctx_count // 2 * DH
            and ctx_count == 16
        )

    def chosen(*args):
        if not by_pairs(args):
            return body(*args)
        return body_by_pairs(*args)

    placed = (
        P(("groups", "ctx"), None),
        P(("groups", "ctx"), None),
        P(("groups", "ctx"), None),
        P(("groups", "ctx"), None),
        P(),
        P(),
        P(None, "ctx"),
        P(None, "ctx"),
        P(),
        P(("groups", "ctx"), None),
        P("ctx", None, None),
        P("ctx", None, None),
    )
    return jax.shard_map(
        chosen, mesh=mesh, in_specs=placed, out_specs=P(("groups", "ctx"), None), check_vma=False
    )
```
